32 devices in a mesh: group: 2 (over y), attn: 4 (over z), sect: 2 (over x), pair: 2 (over core).
Axes of the slice: x: 2, y: 2, z: 4, core: 2. Of those that a mesh axis runs over, the one named last changes fastest.
Arguments:
- queries: bfloat16 [512, 4096], P(('group', 'attn'), ('sect', 'pair')), parts along dimension 0, may hold values from -200 to 200
- kv_pool: bfloat16 [4, 8, 128, 256], P('sect', ('group', 'attn')), parts along dimension 1, may hold values from -8 to 8
- block_list: int32 [8, 2], P(('group', 'attn')), parts along dimension 0, may hold values from 0 to 3, as said below
- cache_len: int32 [8], P(('group', 'attn')), parts along dimension 0, may hold values from 128 to 256, as said below
- out_weight: bfloat16 [4096, 2048], P(('sect', 'pair'), 'attn'), may hold values from -0.09375 to 0.09375
- residual: bfloat16 [512, 2048], P(('group', 'attn', 'sect', 'pair')), parts along dimension 0, may hold values from -4 to 4
- norm_gain: float32 [2048], replicated, may hold values from 0.1 to 1.9
- router: bfloat16 [2048, 8], replicated, may hold values from -50 to 50
- expert_ids: int32 [512, 4], P(('group', 'attn', 'sect', 'pair')), parts along dimension 0, may hold values from 0 to 7, all different within a row; in each aligned block of 16 rows (0 to 15, 16 to 31, ...) at most 16 rows name the same one
- w_gate: bfloat16 [8, 2048, 768], P(('attn', 'pair'), None, 'sect'), may hold values from -0.125 to 0.125
- w_up: bfloat16 [8, 2048, 768], P(('attn', 'pair'), None, 'sect'), may hold values from -0.125 to 0.125
- w_down: bfloat16 [8, 768, 2048], P(('attn', 'pair'), None, 'sect'), may hold values from -0.21875 to 0.21875
Outputs:
- layer_out: bfloat16 [512, 2048], P(('group', 'attn', 'sect', 'pair')), parts along dimension 0
The draws below stay inside these ranges and needn't reach their ends.
There are 2 independent parts, one for each index of `group`. The reference program is written for one: setup_inputs(seed, part) draws one part's arguments, and reference() takes and returns one part's arrays. A program takes and returns all parts, laid end to end along the dimension named above; an argument that names none is the same for every part. Nothing has to cross between parts.
Inputs may be any that keep to these rules, and one draw needn't show every extreme that they name: `block_list`: A group's 2 blocks are distinct, and every block of the pool is listed by some group. `cache_len`: some group has 256 live positions and some group 128. `expert_ids`: each row names 4 different experts; among the rows of one device no expert is named by more than 16 rows, a bound that some block reaches.
All inputs are finite; a program needn't handle non-finite values.
Results may differ from the reference program's by a relative error of at most 0.013.
Values may be sent and summed in bfloat16 or wider, within the bound.
No kernel may reach another device: no remote copies, remote signals or barrier semaphores. Data moves between devices by JAX's collectives and lax.ppermute only.
A program may use at most 64 MiB of HBM per device.

```python
import math
import jax
import jax.numpy as jnp
import numpy as np
from jax import lax

D = 2048
HEADS = 32
KV_HEADS = 4
HEAD_DIM = 128
FF = 768
BLOCK_KEYS = 128
ROW_DEV = 16
EXPERTS = 8
TOPK = 4
CAP = 16
NPOOL = 4
LIST = 2
GROUPS = 4
ROWS_GROUP = 64
TOKENS = 256


def block_lists(base_key):
    pool_order = jax.random.permutation(jax.random.fold_in(base_key, 101), NPOOL)
    base_index = (jnp.arange(GROUPS)[:, None] * LIST + jnp.arange(LIST)[None, :]) % NPOOL
    chosen = pool_order[base_index]
    shuffle_scores = jax.random.randint(jax.random.fold_in(base_key, 102), (GROUPS, LIST), 0, 1 << 20) * LIST + jnp.arange(LIST)[None, :]
    places = jnp.argsort(shuffle_scores, axis=1)
    return jnp.take_along_axis(chosen, places, axis=1).astype(jnp.int32)


def pool_values(base_key):
    pool_shape = (KV_HEADS, NPOOL, BLOCK_KEYS, 2 * HEAD_DIM)
    pool_data = jax.random.truncated_normal(jax.random.fold_in(base_key, 106), -6.0, 6.0, pool_shape, jnp.float32)
    return pool_data


def draw_block_list(key, part):
    return block_lists(key)


def draw_cache_len(key, part):
    lengths = jax.random.randint(jax.random.fold_in(key, 103), (GROUPS,), BLOCK_KEYS, LIST * BLOCK_KEYS + 1)
    longest = jax.random.randint(jax.random.fold_in(key, 104), (), 0, GROUPS)
    shortest = (longest + 1 + jax.random.randint(jax.random.fold_in(key, 105), (), 0, GROUPS - 1)) % GROUPS
    lengths = lengths.at[longest].set(LIST * BLOCK_KEYS).at[shortest].set(BLOCK_KEYS)
    return lengths.astype(jnp.int32)


def draw_kv_pool(key, part):
    return pool_values(key).astype(jnp.bfloat16)


def draw_queries(key, part):
    query_shape = (TOKENS, HEADS * HEAD_DIM)
    query_data = 2.0 * jax.random.truncated_normal(jax.random.fold_in(key, 107), -4.0, 4.0, query_shape, jnp.float32)
    return query_data.astype(jnp.bfloat16)


def draw_router(key, part):
    router_data = jax.random.truncated_normal(jax.random.fold_in(key, 110), -4.0, 4.0, (D, EXPERTS), jnp.float32) / D ** 0.5
    return router_data.astype(jnp.bfloat16)


def levels(own_key, shape, pieces, smallest, top_value):
    loudness = 1.0
    for position, parts in pieces:
        steps = jax.random.uniform(jax.random.fold_in(jax.random.fold_in(own_key, 6), position), (parts,), jnp.float32, smallest / len(pieces), top_value / len(pieces))
        loudness = loudness * jnp.repeat(jnp.exp(steps), shape[position] // parts).reshape((-1,) + (1,) * (len(shape) - 1 - position))
    return loudness


def assign_block(stream_key, own, number, rows, number_of, top, bound, lean):
    ranking = jax.random.permutation(stream_key, number_of)
    packed, ordinary = portions_of(number_of, rows * top, bound, lean, True), portions_of(number_of, rows * top, bound, lean, False)
    places = jnp.arange(number_of)

    def named(sizes, turn):
        used = int((sizes > 0).sum())
        fixed = max(1, used // 4)
        shifted = fixed + (places - fixed + turn * (used - fixed)) % max(1, number_of - fixed)
        return jnp.zeros((number_of,), jnp.int32).at[ranking[jnp.where(places < fixed, places, shifted)]].set(jnp.asarray(sizes, jnp.int32))

    sizes = jnp.where(number % 4 == 0, named(packed, number // 4), named(ordinary, number - number // 4 - 1))
    mixed = jax.random.permutation(jax.random.fold_in(own, 3), number_of)
    source_of, receiver = mixed[0:number_of // 2 * 2:2], mixed[1:number_of // 2 * 2:2]
    slack = jnp.minimum(sizes[source_of] - 1, bound - sizes[receiver]) // 2
    slack = jnp.where((source_of == ranking[0]) | (receiver == ranking[0]) | (sizes[receiver] == 0), 0, jnp.maximum(slack, 0))
    shifted = jax.random.randint(jax.random.fold_in(own, 4), (number_of // 2,), 0, 1 << 20) % (slack + 1)
    sizes = sizes.at[source_of].add(-shifted).at[receiver].add(shifted)
    labels = jnp.searchsorted(jnp.cumsum(sizes), jnp.arange(rows * top), side="right").astype(jnp.int32)
    table = labels.reshape(top, rows).T
    table = table[jax.random.permutation(jax.random.fold_in(own, 1), rows)]
    turn = jax.random.randint(jax.random.fold_in(own, 2), (rows, 1), 0, top)
    return jnp.take_along_axis(table, (jnp.arange(top)[None, :] + turn) % top, axis=1)


def portions_of(count, total, limit, skew, full):
    loads = [(1 << 20) // math.isqrt(standing ** skew) + 1 for standing in range(1, count + 1)]
    largest = limit if full else min(limit, max(-(-total // count), total * loads[0] // sum(loads)))
    least = 1 if total - largest >= count - 1 else 0
    counts, spare = [largest] + [least] * (count - 1), total - largest - least * (count - 1)
    while spare > 0:
        movable = [i for i in range(1, count) if counts[i] < largest] or [i for i in range(1, count) if counts[i] < limit]
        whole, remaining = sum([loads[i] for i in movable]), spare
        for i in movable:
            more = min(limit - counts[i], max(1, remaining * loads[i] // whole), spare)
            counts[i] = counts[i] + more
            spare = spare - more
    return np.array(counts)


def centred(rng, dims, width, bound, cuts=(), held_as=jnp.bfloat16):
    array = jax.random.normal(rng, dims, jnp.float32) * width
    if len(cuts) > 0:
        array = levels(rng, dims, cuts, -0.22, 0.18) * array
    return jnp.clip(array, min=-bound, max=bound).astype(held_as)


def setup_inputs(seed: int = 0, part: int = 0) -> dict:
    key_list = jax.random.split(jax.random.key(seed), 13)
    part_keys = jax.random.split(jax.random.fold_in(key_list[12], part), 13)
    queries = draw_queries(jax.random.fold_in(jax.random.fold_in(key_list[12], part), 71), part)
    kv_pool = draw_kv_pool(jax.random.fold_in(jax.random.fold_in(key_list[12], part), 71), part)
    block_list = draw_block_list(jax.random.fold_in(jax.random.fold_in(key_list[12], part), 71), part)
    cache_len = draw_cache_len(jax.random.fold_in(jax.random.fold_in(key_list[12], part), 71), part)
    out_weight = centred(key_list[4], (HEADS * HEAD_DIM, D), (HEADS * HEAD_DIM) ** -0.5, 0.09375, ((0, 4), (1, 4)))
    residual = centred(part_keys[5], (TOKENS, D), 0.3, 4.0, ((0, 16),))
    norm_gain = jnp.clip(1.0 + 0.18 * jax.random.normal(key_list[6], (D,), jnp.float32), 0.1, 1.9)
    router = draw_router(jax.random.fold_in(key_list[12], 71), part)
    expert_ids_keys = jax.random.split(jax.random.fold_in(part_keys[8], 1), TOKENS // ROW_DEV)
    expert_ids_turns = jax.random.permutation(jax.random.fold_in(part_keys[8], 3), TOKENS // ROW_DEV)
    expert_ids = jax.vmap(lambda own, number: assign_block(jax.random.fold_in(part_keys[8], 2), own, number, ROW_DEV, EXPERTS, TOPK, CAP, 2))(expert_ids_keys, expert_ids_turns).reshape((TOKENS, TOPK))
    w_gate = centred(key_list[9], (EXPERTS, D, FF), D ** -0.5, 0.125, ((0, 8), (2, 2)))
    w_up = centred(key_list[10], (EXPERTS, D, FF), D ** -0.5, 0.125, ((0, 8), (2, 2)))
    w_down = centred(key_list[11], (EXPERTS, FF, D), FF ** -0.5, 0.21875, ((0, 8), (2, 2)))
    return {"queries": queries, "kv_pool": kv_pool, "block_list": block_list, "cache_len": cache_len, "out_weight": out_weight, "residual": residual, "norm_gain": norm_gain, "router": router, "expert_ids": expert_ids, "w_gate": w_gate, "w_up": w_up, "w_down": w_down}


def attend_group(group, queries, kv_pool, block_list, cache_len):
    head_dim = HEAD_DIM
    per_kv = HEADS // KV_HEADS
    row_block = lax.dynamic_slice_in_dim(queries, (group * ROWS_GROUP).astype(jnp.int32), ROWS_GROUP, 0)
    row_block = row_block.astype(jnp.float32).reshape(ROWS_GROUP, KV_HEADS, per_kv, head_dim)
    listed = jnp.take(kv_pool, block_list[group], axis=1)
    listed = listed.reshape(KV_HEADS, LIST * BLOCK_KEYS, 2 * head_dim).astype(jnp.float32)
    key_rows = listed[:, :, :head_dim]
    values = listed[:, :, head_dim:]
    scores = jnp.einsum('rkgd,ktd->rkgt', row_block, key_rows) / math.sqrt(head_dim)
    live_mask = jnp.arange(LIST * BLOCK_KEYS) < cache_len[group]
    scores = jnp.where(live_mask, scores, -jnp.inf)
    row_top = lax.optimization_barrier(jnp.max(scores, axis=-1, keepdims=True))
    lifted = jnp.exp(scores - row_top)
    row_total = lax.optimization_barrier(jnp.sum(lifted, axis=-1))
    soft_weights = lax.optimization_barrier(lifted.astype(jnp.bfloat16)).astype(jnp.float32)
    mixed_heads = jnp.einsum('rkgt,ktd->rkgd', soft_weights, values) / row_total[..., None]
    return mixed_heads.reshape(ROWS_GROUP, HEADS * head_dim).astype(jnp.bfloat16)

def expert_step(operands):
    buffer, gate_part, up_part, down_part = operands
    gate_val = jnp.dot(buffer, gate_part, preferred_element_type=jnp.float32)
    up_val = jnp.dot(buffer, up_part, preferred_element_type=jnp.float32)
    hidden = (jax.nn.silu(gate_val) * up_val).astype(jnp.bfloat16)
    return jnp.dot(hidden, down_part, preferred_element_type=jnp.float32).astype(jnp.bfloat16)

def reference(queries, kv_pool, block_list, cache_len, out_weight, residual, norm_gain, router, expert_ids, w_gate, w_up, w_down):
    attended = lax.map(lambda group: attend_group(group, queries, kv_pool, block_list, cache_len), jnp.arange(GROUPS, dtype=jnp.int32))
    attended = attended.reshape(TOKENS, HEADS * HEAD_DIM)
    mixed_rows = (residual.astype(jnp.float32) + jnp.dot(attended, out_weight, preferred_element_type=jnp.float32)).astype(jnp.bfloat16)
    mixed_f32 = mixed_rows.astype(jnp.float32)
    normed = (mixed_f32 * lax.rsqrt(lax.optimization_barrier(jnp.mean(mixed_f32 * mixed_f32, axis=-1, keepdims=True)) + 1e-06) * norm_gain).astype(jnp.bfloat16)
    logits = jnp.dot(normed, router, preferred_element_type=jnp.float32)
    chosen_logits = jnp.take_along_axis(logits, expert_ids, axis=1)
    route_weights = jax.nn.softmax(chosen_logits, axis=-1)
    flat_ids = expert_ids.reshape(-1)
    onehot = (flat_ids[:, None] == jnp.arange(EXPERTS, dtype=jnp.int32)[None, :]).astype(jnp.int32)
    earlier = jnp.cumsum(onehot, axis=0) - onehot
    slot_index = lax.optimization_barrier(jnp.sum(earlier * onehot, axis=1)).astype(jnp.int32)
    source = jnp.repeat(jnp.arange(TOKENS, dtype=jnp.int32), TOPK)
    most_slots = TOKENS // ROW_DEV * CAP
    buffer = jnp.zeros((EXPERTS, most_slots, D), jnp.bfloat16).at[flat_ids, slot_index].set(normed[source])
    expert_outs = lax.map(expert_step, (buffer, w_gate, w_up, w_down))
    gathered = expert_outs[flat_ids, slot_index].reshape(TOKENS, TOPK, D).astype(jnp.float32)
    joined = lax.optimization_barrier(jnp.sum(route_weights[:, :, None] * gathered, axis=1))
    return (mixed_f32 + joined).astype(jnp.bfloat16)
```

```python
import functools
import math

import jax
import jax.numpy as jnp
from jax import lax
from jax.experimental import pallas as pl
from jax.experimental.pallas import tpu as pltpu
from jax.sharding import PartitionSpec as P

HEADS = 32
KV_HEADS = 4
HEAD_DIM = 128


VMEM = pl.BlockSpec(memory_space=pltpu.VMEM)
SMEM = pl.BlockSpec(memory_space=pltpu.SMEM)


def routed_layer(
    queries,
    kv_pool,
    block_list,
    cache_len,
    out_weight,
    residual,
    norm_gain,
    router,
    expert_ids,
    w_gate,
    w_up,
    w_down,
):
    head_dim = HEAD_DIM
    per_kv = HEADS // KV_HEADS
    group_rows, head_cols = queries.shape
    local_heads = head_cols // head_dim
    pool_all = lax.all_gather(kv_pool, "attn", axis=1, tiled=True)
    picked = jnp.take(pool_all, block_list[0], axis=1)
    kv_local = lax.axis_index("pair") * local_heads // per_kv
    chosen = lax.dynamic_index_in_dim(picked, kv_local, 0, keepdims=False)
    chosen = chosen.reshape(-1, 2 * head_dim)
    key_rows = chosen[:, :head_dim]
    values = chosen[:, head_dim:]
    query_heads = queries.reshape(group_rows, local_heads, head_dim)
    scores = jnp.einsum(
        "rhd,td->rht", query_heads, key_rows, preferred_element_type=jnp.float32
    ) / math.sqrt(head_dim)
    live_mask = jnp.arange(key_rows.shape[0]) < cache_len[0]
    scores = jnp.where(live_mask, scores, -jnp.inf)
    row_top = jnp.max(scores, axis=-1, keepdims=True)
    lifted = jnp.exp(scores - row_top)
    row_total = jnp.sum(lifted, axis=-1)
    soft_weights = lifted.astype(jnp.bfloat16)
    mixed_heads = (
        jnp.einsum("rht,td->rhd", soft_weights, values, preferred_element_type=jnp.float32)
        / row_total[..., None]
    )
    attended = mixed_heads.reshape(group_rows, head_cols).astype(jnp.bfloat16)
    partial_value = jnp.dot(
        attended,
        lax.all_gather(out_weight, "attn", axis=1, tiled=True),
        preferred_element_type=jnp.float32,
    )
    summed = lax.psum_scatter(partial_value, ("sect", "pair"), scatter_dimension=0, tiled=True)
    mixed_f32 = residual.astype(jnp.float32) + summed
    mixed_rows = mixed_f32.astype(jnp.bfloat16)
    mixed_f32 = mixed_rows.astype(jnp.float32)
    normed = (
        mixed_f32
        * lax.rsqrt(jnp.mean(mixed_f32 * mixed_f32, axis=-1, keepdims=True) + 1e-06)
        * norm_gain
    ).astype(jnp.bfloat16)
    logits = jnp.dot(normed, router, preferred_element_type=jnp.float32)
    chosen_logits = jnp.take_along_axis(logits, expert_ids, axis=1)
    route_weights = jax.nn.softmax(chosen_logits, axis=-1)
    row_count, top_count = expert_ids.shape
    expert_count = router.shape[1]
    model_width = residual.shape[1]
    capacity = max(2, row_count * top_count // expert_count * 2)
    flat_ids = expert_ids.reshape(-1)
    onehot = (flat_ids[:, None] == jnp.arange(expert_count, dtype=jnp.int32)[None, :]).astype(
        jnp.int32
    )
    earlier = jnp.cumsum(onehot, axis=0) - onehot
    slot_index = jnp.sum(earlier * onehot, axis=1)
    source = jnp.repeat(jnp.arange(row_count, dtype=jnp.int32), top_count)
    outgoing = (
        jnp.zeros((expert_count, capacity, model_width), jnp.bfloat16)
        .at[flat_ids, slot_index]
        .set(normed[source])
    )
    received = lax.all_to_all(outgoing, ("attn", "pair"), split_axis=0, concat_axis=0, tiled=True)
    sections = lax.axis_size("sect")
    every_section = lax.all_gather(received, "sect", axis=0, tiled=True)
    tokens_in = every_section.reshape(-1, model_width)
    gate_val = jnp.dot(tokens_in, w_gate[0], preferred_element_type=jnp.float32)
    up_val = jnp.dot(tokens_in, w_up[0], preferred_element_type=jnp.float32)
    part_hidden = (jax.nn.silu(gate_val) * up_val).astype(jnp.bfloat16)
    hidden = lax.all_gather(part_hidden, "sect", axis=1, tiled=True)
    out_slice = jnp.dot(hidden, w_down[0], preferred_element_type=jnp.float32).astype(jnp.bfloat16)
    out_slice = out_slice.reshape(sections, expert_count, capacity, model_width // sections)
    segmented = lax.all_to_all(out_slice, "sect", split_axis=0, concat_axis=3, tiled=True)
    returned = lax.all_to_all(
        segmented[0], ("attn", "pair"), split_axis=0, concat_axis=0, tiled=True
    )
    gathered = (
        returned[flat_ids, slot_index]
        .reshape(row_count, top_count, model_width)
        .astype(jnp.float32)
    )
    joined = jnp.sum(route_weights[:, :, None] * gathered, axis=1)
    return (mixed_f32 + joined).astype(jnp.bfloat16)


def rotate(value, axis, step):
    size = lax.axis_size(axis)
    return lax.ppermute(value, axis, [(i, (i + step) % size) for i in range(size)])


def steps_of(size):
    return sorted(range(1, size), key=lambda k: -min(k, size - k))


def attend_kernel(attn, sect, pair, list_len, per_dev, place_ref, *refs):
    q_refs, refs = refs[:attn], refs[attn:]
    kv_refs, refs = refs[:attn], refs[attn:]
    w_ref, refs = refs[0], refs[1:]
    part_refs, refs = refs[:pair], refs[pair:]
    pool, attended, split = refs
    rows, head_cols = q_refs[0].shape
    heads = head_cols // HEAD_DIM
    blocks = pool.shape[0] // attn
    keys = pool.shape[1]
    me = place_ref[0]
    my_pair = place_ref[2]
    lane = lax.broadcasted_iota(jnp.int32, (1, kv_refs[0].shape[1]), 1)
    lists = []
    for k in range(attn):
        group = lax.rem(me + attn - k, attn)
        for b in range(blocks):
            pool[group * blocks + b] = kv_refs[k][b * keys : (b + 1) * keys, :]
        meta = kv_refs[k][blocks * keys : blocks * keys + 16, :].astype(jnp.float32)[0:1, :]
        lists.append(
            [
                jnp.sum(jnp.where(lane == j, meta, 0.0)).astype(jnp.int32)
                for j in range(list_len)
            ]
            + [
                jnp.sum(jnp.where(lane == list_len, meta * 128.0, 0.0)
                        + jnp.where(lane == list_len + 1, meta, 0.0)).astype(jnp.int32)
            ]
        )
    for k in range(attn):
        group = lax.rem(me + attn - k, attn)
        listed = lists[k][:list_len]
        live = lists[k][list_len]
        picked = [pool[index] for index in listed]
        key_rows = jnp.concatenate([p[:, :HEAD_DIM] for p in picked], axis=0)
        values = jnp.concatenate([p[:, HEAD_DIM:] for p in picked], axis=0)
        q_all = q_refs[k][...]
        stacked = jnp.concatenate(
            [q_all[:, h * HEAD_DIM : (h + 1) * HEAD_DIM] for h in range(heads)], axis=0
        )
        scores = lax.dot_general(
            stacked, key_rows, (((1,), (1,)), ((), ())), preferred_element_type=jnp.float32
        ) / math.sqrt(HEAD_DIM)
        where = lax.broadcasted_iota(jnp.int32, scores.shape, 1)
        scores = jnp.where(where < live, scores, -jnp.inf)
        top = jnp.max(scores, axis=-1, keepdims=True)
        lifted = jnp.exp(scores - top)
        total = jnp.sum(lifted, axis=-1, keepdims=True)
        mixed = (
            jnp.dot(lifted.astype(jnp.bfloat16), values, preferred_element_type=jnp.float32)
            / total
        ).astype(jnp.bfloat16)
        start = pl.multiple_of(group * rows, rows)
        for h in range(heads):
            attended[pl.ds(start, rows), h * HEAD_DIM : (h + 1) * HEAD_DIM] = mixed[
                h * rows : (h + 1) * rows, :
            ]
    product = jnp.dot(attended[...], w_ref[...], preferred_element_type=jnp.float32)
    for g in range(attn):
        for s in range(sect):
            for p in range(pair):
                source = g * rows + (s * pair + p) * per_dev
                target = (s * attn + g) * per_dev
                split[p, target : target + per_dev, :] = product[source : source + per_dev, :]
    for i in range(pair):
        part_refs[i][...] = split[lax.rem(my_pair + i, pair)]


def expert_kernel(attn, sect, pair, per_dev, top, place_ref, *refs):
    piece_refs, refs = refs[: attn * pair], refs[attn * pair :]
    side_refs, refs = refs[:attn], refs[attn:]
    gain_ref, router_ref, gate_ref, up_ref, down_ref, refs = *refs[:5], refs[5:]
    other_down, refs = refs[: sect - 1], refs[sect - 1 :]
    part_refs, refs = refs[:pair], refs[pair:]
    own_ref, ids_all, contribution = refs
    half, width = piece_refs[0].shape
    model = width * attn
    me, my_sect, my_expert = place_ref[0], place_ref[1], place_ref[3]
    rows = half * pair
    for k in range(attn):
        group = lax.rem(me + attn - k, attn)
        block = side_refs[k][:, width:].astype(jnp.float32)
        for i in range(sect):
            from_sect = lax.rem(my_sect + sect - i, sect)
            start = (from_sect * attn + group) * per_dev
            for j in range(pair):
                lane = (i * pair + j) * top
                ids_all[pl.ds(pl.multiple_of(j * half + start, per_dev), per_dev), :] = block[
                    :, lane : lane + top
                ]
    values = []
    squares = jnp.zeros((rows, 1), jnp.float32)
    for k in range(attn):
        value = jnp.concatenate(
            [piece_refs[j * attn + k][...] for j in range(pair)], axis=0
        ).astype(jnp.float32)
        values.append(value)
        squares = squares + jnp.sum(value * value, axis=-1, keepdims=True)
    scale = lax.rsqrt(squares / model + 1e-06)
    gate = up = logits = None
    own_start = pl.multiple_of((my_sect * attn + me) * per_dev, per_dev)
    for k in range(attn):
        group = lax.rem(me + attn - k, attn)
        cols = pl.ds(pl.multiple_of(group * width, width), width)
        normed = (values[k] * scale * gain_ref[pl.ds(group, 1), :]).astype(jnp.bfloat16)
        parts = [
            jnp.dot(normed, ref[cols, :], preferred_element_type=jnp.float32)
            for ref in (gate_ref, up_ref, router_ref)
        ]
        if k == 0:
            gate, up, logits = parts
        else:
            gate, up, logits = gate + parts[0], up + parts[1], logits + parts[2]
        own_ref[:, cols] = piece_refs[k][pl.ds(own_start, per_dev), :]
    ids = ids_all[...]
    lane = lax.broadcasted_iota(jnp.int32, logits.shape, 1)
    lane_f = lane.astype(jnp.float32)
    named = lane < 0
    for c in range(top):
        named = named | (ids[:, c : c + 1] == lane_f)
    chosen = jnp.where(named, logits, -jnp.inf)
    lifted = jnp.exp(chosen - jnp.max(chosen, axis=-1, keepdims=True))
    weights = lifted / jnp.sum(lifted, axis=-1, keepdims=True)
    weight = jnp.sum(jnp.where(lane == my_expert, weights, 0.0), axis=-1, keepdims=True)
    hidden = (gate / (1.0 + jnp.exp(-gate)) * up).astype(jnp.bfloat16)
    ff = hidden.shape[1]
    section = down_ref.shape[1]
    own_down = down_ref[pl.ds(pl.multiple_of(my_sect * ff, ff), ff), :]
    for i in range(sect):
        matrix = own_down if i == 0 else other_down[i - 1][...]
        from_sect = lax.rem(my_sect + sect - i, sect)
        cols = pl.ds(pl.multiple_of(from_sect * section, section), section)
        contribution[:, cols] = (
            jnp.dot(hidden, matrix, preferred_element_type=jnp.float32) * weight
        )
    part_refs[0][...] = contribution[:half, :]
    for j in range(1, pair):
        part_refs[j][...] = contribution[j * half : (j + 1) * half, :].astype(jnp.bfloat16)


def sect_split_kernel(sect, count, place_ref, kept_ref, *refs):
    came, outs = refs[:count], refs[count:]
    part = kept_ref.shape[0] // sect
    for i in range(sect):
        rows = pl.ds(pl.multiple_of(lax.rem(place_ref[1] + i, sect) * part, part), part)
        total = kept_ref[rows, :]
        for ref in came:
            total = total + ref[rows, :].astype(jnp.float32)
        outs[i][...] = total.astype(outs[i].dtype)


def attn_split_kernel(attn, count, place_ref, kept_ref, *refs):
    came, outs = refs[:count], refs[count:]
    part = kept_ref.shape[0] // attn
    for i in range(attn):
        rows = pl.ds(pl.multiple_of(lax.rem(place_ref[0] + i, attn) * part, part), part)
        total = kept_ref[rows, :]
        for ref in came:
            total = total + ref[rows, :].astype(jnp.float32)
        outs[i][...] = total.astype(outs[i].dtype)


def call(kernel, place, operands, outs, scratch=(), limit=None, flops=1 << 20):
    moved = sum(x.size * x.dtype.itemsize for x in operands)
    return pl.pallas_call(
        kernel,
        out_shape=outs,
        in_specs=[SMEM] + [VMEM] * len(operands),
        out_specs=jax.tree.map(lambda _: VMEM, outs),
        scratch_shapes=list(scratch),
        compiler_params=pltpu.CompilerParams(vmem_limit_bytes=limit),
        cost_estimate=pl.CostEstimate(flops=flops, bytes_accessed=moved, transcendentals=0),
    )(place, *operands)


def dense_layer(
    queries,
    kv_pool,
    block_list,
    cache_len,
    out_weight,
    residual,
    norm_gain,
    router,
    expert_ids,
    w_gate,
    w_up,
    w_down,
):
    attn, sect, pair = (lax.axis_size(n) for n in ("attn", "sect", "pair"))
    my_attn, my_sect, my_pair = (lax.axis_index(n) for n in ("attn", "sect", "pair"))
    bf16, f32 = jnp.bfloat16, jnp.float32
    rows, head_cols = queries.shape
    local_heads = head_cols // HEAD_DIM
    per_kv = HEADS // KV_HEADS
    per_dev, model = residual.shape
    top = expert_ids.shape[1]
    width = out_weight.shape[1]
    ff = w_gate.shape[2]
    list_len = block_list.shape[1]
    _, blocks, keys, kv_cols = kv_pool.shape
    half = attn * sect * per_dev
    place = jnp.stack([my_attn, my_sect, my_pair, my_attn * pair + my_pair]).astype(jnp.int32)

    kv_local = my_pair * local_heads // per_kv
    own_kv = lax.dynamic_index_in_dim(kv_pool, kv_local, 0, keepdims=False)
    own_kv = own_kv.reshape(blocks * keys, kv_cols)
    facts = jnp.concatenate([block_list[0], cache_len // 128, cache_len % 128]).astype(bf16)
    facts = jnp.zeros((16, kv_cols), bf16).at[0, : list_len + 2].set(facts)
    own_kv = jnp.concatenate([own_kv, facts], axis=0)
    kv = {0: own_kv}
    q = {0: queries}
    for k in steps_of(attn):
        kv[k] = rotate(own_kv, "attn", k)
    for k in steps_of(attn):
        q[k] = rotate(queries, "attn", k)

    ids = [expert_ids.astype(bf16)]
    ids += [rotate(ids[0], "pair", j) for j in range(1, pair)]
    ids = jnp.concatenate(ids, axis=1)
    ids = [ids] + [rotate(ids, "sect", i) for i in range(1, sect)]
    ids = jnp.concatenate(ids, axis=1)
    lanes = -(-ids.shape[1] // 128) * 128
    ids = jnp.pad(ids, ((0, 0), (0, lanes - ids.shape[1])))

    def side_for(k):
        start = (my_attn + k) % attn * width
        return jnp.concatenate(
            [lax.dynamic_slice_in_dim(residual, start, width, 1), ids], axis=1
        )

    side = {0: side_for(0)}
    for k in steps_of(attn):
        side[k] = rotate(side_for(k), "attn", k)

    other_down = []
    for i in range(1, sect):
        start = (my_sect + i) % sect * ff
        other_down.append(
            rotate(lax.dynamic_slice_in_dim(w_down[0], start, ff, 0), "sect", i)
        )

    parts = call(
        functools.partial(attend_kernel, attn, sect, pair, list_len, per_dev),
        place,
        [q[k] for k in range(attn)] + [kv[k] for k in range(attn)] + [out_weight],
        [jax.ShapeDtypeStruct((half, width), f32)] * pair,
        [
            pltpu.VMEM((attn * blocks, keys, kv_cols), bf16),
            pltpu.VMEM((attn * rows, head_cols), bf16),
            pltpu.VMEM((pair, half, width), f32),
        ],
        limit=16 << 20,
    )
    total = parts[0]
    for j in range(1, pair):
        total = total + rotate(parts[j], "pair", j)
    res = jnp.concatenate(
        [side[k][None, :, :width] for k in range(attn)], axis=0
    )
    order = (my_attn - jnp.arange(attn)) % attn
    res = jnp.stack([lax.dynamic_index_in_dim(res, order[g], 0, keepdims=False) for g in range(attn)])
    res = res.reshape(1, attn * per_dev, width).astype(f32)
    mine = (jnp.arange(sect) == my_sect)[:, None, None]
    total = (total.reshape(sect, attn * per_dev, width) + jnp.where(mine, res, 0.0)).reshape(
        half, width
    )
    sent = total.astype(bf16)
    for i in range(1, sect):
        total = total + rotate(sent, "sect", i).astype(f32)
    mixed = total.astype(bf16)
    piece = {0: mixed}
    for k in steps_of(attn):
        piece[k] = rotate(mixed, "attn", k)
    pieces = [piece[k] for k in range(attn)]
    for j in range(1, pair):
        pieces += [rotate(piece[k], "pair", j) for k in range(attn)]

    outs = call(
        functools.partial(expert_kernel, attn, sect, pair, per_dev, top),
        place,
        pieces
        + [side[k] for k in range(attn)]
        + [norm_gain.reshape(attn, width), router, w_gate[0], w_up[0], w_down[0]]
        + other_down,
        [jax.ShapeDtypeStruct((half, model), f32)]
        + [jax.ShapeDtypeStruct((half, model), bf16)] * (pair - 1)
        + [jax.ShapeDtypeStruct((per_dev, model), bf16)],
        [
            pltpu.VMEM((half * pair, top), f32),
            pltpu.VMEM((half * pair, model), f32),
        ],
        limit=24 << 20,
    )
    own_mixed = outs[pair]
    came = [rotate(outs[j], "pair", pair - j) for j in range(1, pair)]
    part = half // sect
    outs = call(
        functools.partial(sect_split_kernel, sect, pair - 1),
        place,
        [outs[0]] + came,
        [jax.ShapeDtypeStruct((part, model), f32)]
        + [jax.ShapeDtypeStruct((part, model), bf16)] * (sect - 1),
        limit=8 << 20,
    )
    came = [rotate(outs[i], "sect", i) for i in range(1, sect)]
    outs = call(
        functools.partial(attn_split_kernel, attn, sect - 1),
        place,
        [outs[0]] + came,
        [jax.ShapeDtypeStruct((per_dev, model), f32)]
        + [jax.ShapeDtypeStruct((per_dev, model), bf16)] * (attn - 1),
        limit=8 << 20,
    )
    total = own_mixed.astype(f32) + outs[0]
    for k in steps_of(attn):
        total = total + rotate(outs[k], "attn", k).astype(f32)
    return total.astype(bf16)


def on_device(*operands):
    queries, expert_ids, router = operands[0], operands[8], operands[7]
    row_count, top_count = expert_ids.shape
    capacity = max(2, row_count * top_count // router.shape[1] * 2)
    local_heads = queries.shape[1] // HEAD_DIM
    one_each = operands[9].shape[0] == 1
    if capacity >= row_count and one_each and local_heads <= HEADS // KV_HEADS:
        return dense_layer(*operands)
    return routed_layer(*operands)


def solution(mesh):
    placed = (
        P(("group", "attn"), ("sect", "pair")),
        P("sect", ("group", "attn"), None, None),
        P(("group", "attn"), None),
        P(("group", "attn")),
        P(("sect", "pair"), "attn"),
        P(("group", "attn", "sect", "pair"), None),
        P(),
        P(),
        P(("group", "attn", "sect", "pair"), None),
        P(("attn", "pair"), None, "sect"),
        P(("attn", "pair"), None, "sect"),
        P(("attn", "pair"), None, "sect"),
    )
    return jax.shard_map(
        on_device,
        mesh=mesh,
        in_specs=placed,
        out_specs=P(("group", "attn", "sect", "pair"), None),
        check_vma=False,
    )
```

```python
import functools
import math

import jax
import jax.numpy as jnp
from jax import lax
from jax.experimental import pallas as pl
from jax.experimental.pallas import tpu as pltpu
from jax.sharding import PartitionSpec as P

HEADS = 32
KV_HEADS = 4
HEAD_DIM = 128


VMEM = pl.BlockSpec(memory_space=pltpu.VMEM)


def routed_layer(
    queries,
    kv_pool,
    block_list,
    cache_len,
    out_weight,
    residual,
    norm_gain,
    router,
    expert_ids,
    w_gate,
    w_up,
    w_down,
):
    head_dim = HEAD_DIM
    per_kv = HEADS // KV_HEADS
    group_rows, head_cols = queries.shape
    local_heads = head_cols // head_dim
    pool_all = lax.all_gather(kv_pool, "attn", axis=1, tiled=True)
    picked = jnp.take(pool_all, block_list[0], axis=1)
    kv_local = lax.axis_index("pair") * local_heads // per_kv
    chosen = lax.dynamic_index_in_dim(picked, kv_local, 0, keepdims=False)
    chosen = chosen.reshape(-1, 2 * head_dim)
    key_rows = chosen[:, :head_dim]
    values = chosen[:, head_dim:]
    query_heads = queries.reshape(group_rows, local_heads, head_dim)
    scores = jnp.einsum(
        "rhd,td->rht", query_heads, key_rows, preferred_element_type=jnp.float32
    ) / math.sqrt(head_dim)
    live_mask = jnp.arange(key_rows.shape[0]) < cache_len[0]
    scores = jnp.where(live_mask, scores, -jnp.inf)
    row_top = jnp.max(scores, axis=-1, keepdims=True)
    lifted = jnp.exp(scores - row_top)
    row_total = jnp.sum(lifted, axis=-1)
    soft_weights = lifted.astype(jnp.bfloat16)
    mixed_heads = (
        jnp.einsum("rht,td->rhd", soft_weights, values, preferred_element_type=jnp.float32)
        / row_total[..., None]
    )
    attended = mixed_heads.reshape(group_rows, head_cols).astype(jnp.bfloat16)
    partial_value = jnp.dot(
        attended,
        lax.all_gather(out_weight, "attn", axis=1, tiled=True),
        preferred_element_type=jnp.float32,
    )
    summed = lax.psum_scatter(partial_value, ("sect", "pair"), scatter_dimension=0, tiled=True)
    mixed_f32 = residual.astype(jnp.float32) + summed
    mixed_rows = mixed_f32.astype(jnp.bfloat16)
    mixed_f32 = mixed_rows.astype(jnp.float32)
    normed = (
        mixed_f32
        * lax.rsqrt(jnp.mean(mixed_f32 * mixed_f32, axis=-1, keepdims=True) + 1e-06)
        * norm_gain
    ).astype(jnp.bfloat16)
    logits = jnp.dot(normed, router, preferred_element_type=jnp.float32)
    chosen_logits = jnp.take_along_axis(logits, expert_ids, axis=1)
    route_weights = jax.nn.softmax(chosen_logits, axis=-1)
    row_count, top_count = expert_ids.shape
    expert_count = router.shape[1]
    model_width = residual.shape[1]
    capacity = max(2, row_count * top_count // expert_count * 2)
    flat_ids = expert_ids.reshape(-1)
    onehot = (flat_ids[:, None] == jnp.arange(expert_count, dtype=jnp.int32)[None, :]).astype(
        jnp.int32
    )
    earlier = jnp.cumsum(onehot, axis=0) - onehot
    slot_index = jnp.sum(earlier * onehot, axis=1)
    source = jnp.repeat(jnp.arange(row_count, dtype=jnp.int32), top_count)
    outgoing = (
        jnp.zeros((expert_count, capacity, model_width), jnp.bfloat16)
        .at[flat_ids, slot_index]
        .set(normed[source])
    )
    received = lax.all_to_all(outgoing, ("attn", "pair"), split_axis=0, concat_axis=0, tiled=True)
    sections = lax.axis_size("sect")
    every_section = lax.all_gather(received, "sect", axis=0, tiled=True)
    tokens_in = every_section.reshape(-1, model_width)
    gate_val = jnp.dot(tokens_in, w_gate[0], preferred_element_type=jnp.float32)
    up_val = jnp.dot(tokens_in, w_up[0], preferred_element_type=jnp.float32)
    part_hidden = (jax.nn.silu(gate_val) * up_val).astype(jnp.bfloat16)
    hidden = lax.all_gather(part_hidden, "sect", axis=1, tiled=True)
    out_slice = jnp.dot(hidden, w_down[0], preferred_element_type=jnp.float32).astype(jnp.bfloat16)
    out_slice = out_slice.reshape(sections, expert_count, capacity, model_width // sections)
    segmented = lax.all_to_all(out_slice, "sect", split_axis=0, concat_axis=3, tiled=True)
    returned = lax.all_to_all(
        segmented[0], ("attn", "pair"), split_axis=0, concat_axis=0, tiled=True
    )
    gathered = (
        returned[flat_ids, slot_index]
        .reshape(row_count, top_count, model_width)
        .astype(jnp.float32)
    )
    joined = jnp.sum(route_weights[:, :, None] * gathered, axis=1)
    return (mixed_f32 + joined).astype(jnp.bfloat16)


def rotate(value, axis, step):
    size = lax.axis_size(axis)
    return lax.ppermute(value, axis, [(i, (i + step) % size) for i in range(size)])


def steps_of(size):
    return sorted(range(1, size), key=lambda k: -min(k, size - k))


def pack_kernel(attn, kv_ref, list_ref, len_ref, res_ref, ids_ref, *packs):
    my_attn = lax.axis_index("attn")
    head_cols = packs[0].shape[1]
    per_dev = res_ref.shape[0]
    top = ids_ref.shape[0]
    width = res_ref.shape[1] // attn
    _, blocks, keys, kv_cols = kv_ref.shape
    folds = head_cols // kv_cols
    low = blocks * keys // folds
    local_heads = head_cols // HEAD_DIM
    kv_local = lax.axis_index("pair") * local_heads // (HEADS // KV_HEADS)
    lane = lax.broadcasted_iota(jnp.int32, (per_dev, 128), 1)
    facts = jnp.zeros((per_dev, 128), jnp.int32)
    list_len = list_ref.shape[1]
    for j in range(list_len):
        facts = jnp.where(lane == j, list_ref[:, j : j + 1], facts)
    facts = jnp.where(lane == list_len, len_ref[...] // 128, facts)
    facts = jnp.where(lane == list_len + 1, lax.rem(len_ref[...], 128), facts)
    facts = facts.astype(jnp.float32).astype(jnp.bfloat16)
    eye = (
        lax.broadcasted_iota(jnp.int32, (per_dev, per_dev), 0)
        == lax.broadcasted_iota(jnp.int32, (per_dev, per_dev), 1)
    )
    ids = lax.dot_general(
        eye.astype(jnp.float32).astype(jnp.bfloat16),
        ids_ref[...].astype(jnp.float32).astype(jnp.bfloat16),
        (((1,), (1,)), ((), ())),
        preferred_element_type=jnp.float32,
    )
    ids = jnp.concatenate([ids, jnp.zeros((per_dev, 128 - top), jnp.float32)], axis=1)
    ids = ids.astype(jnp.bfloat16)
    for k in range(attn):
        for f in range(folds):
            block, first = divmod(f * low, keys)
            packs[k][0:low, f * kv_cols : (f + 1) * kv_cols] = kv_ref[
                kv_local, block, first : first + low, :
            ]
        start = pl.multiple_of(lax.rem(my_attn + k, attn) * width, width)
        packs[k][low : low + per_dev, 0:width] = res_ref[:, pl.ds(start, width)]
        packs[k][low : low + per_dev, width : width + 128] = ids
        packs[k][low : low + per_dev, width + 128 : width + 256] = facts
        if width + 256 < head_cols:
            packs[k][low : low + per_dev, width + 256 :] = jnp.zeros(
                (per_dev, head_cols - width - 256), jnp.bfloat16
            )


def halves_kernel(sect, down_ref, *outs):
    my_sect = lax.axis_index("sect")
    ff = outs[0].shape[0]
    for i in range(sect):
        start = pl.multiple_of(lax.rem(my_sect + i, sect) * ff, ff)
        outs[i][...] = down_ref[pl.ds(start, ff), :]


def attend_kernel(attn, sect, pair, list_len, rows, blocks, keys, kv_cols, *refs):
    q_refs, refs = refs[:attn], refs[attn:]
    pack_refs, refs = refs[:attn], refs[attn:]
    w_ref, refs = refs[0], refs[1:]
    part_refs, refs = refs[:pair], refs[pair:]
    ids_ref, pool, attended, split = refs
    per_dev = ids_ref.shape[0]
    head_cols = pack_refs[0].shape[1]
    width = w_ref.shape[1]
    heads = head_cols // HEAD_DIM
    folds = head_cols // kv_cols
    kv_rows = blocks * keys // folds
    me, my_sect, my_pair = (lax.axis_index(n) for n in ("attn", "sect", "pair"))
    low = kv_rows
    lane = lax.broadcasted_iota(jnp.int32, (1, 128), 1)
    lists, lives = [], []
    for k in range(attn):
        group = lax.rem(me + attn - k, attn)
        for f in range(folds):
            block, first = divmod(f * kv_rows, keys)
            pool[group * blocks + block, first : first + kv_rows, :] = pack_refs[k][
                0:kv_rows, f * kv_cols : (f + 1) * kv_cols
            ]
        facts = pack_refs[k][low : low + per_dev, width + 128 : width + 256]
        facts = facts.astype(jnp.float32)[0:1, :]

        def fact(j, facts=facts):
            return jnp.sum(jnp.where(lane == j, facts, 0.0)).astype(jnp.int32)

        lists.append([fact(j) for j in range(list_len)])
        lives.append(fact(list_len) * 128 + fact(list_len + 1))
    for k in range(attn):
        group = lax.rem(me + attn - k, attn)
        picked = [pool[index] for index in lists[k]]
        key_rows = jnp.concatenate([p[:, :HEAD_DIM] for p in picked], axis=0)
        values = jnp.concatenate([p[:, HEAD_DIM:] for p in picked], axis=0)
        q_all = q_refs[k][...]
        stacked = jnp.concatenate(
            [q_all[:, h * HEAD_DIM : (h + 1) * HEAD_DIM] for h in range(heads)], axis=0
        )
        scores = lax.dot_general(
            stacked, key_rows, (((1,), (1,)), ((), ())), preferred_element_type=jnp.float32
        ) / math.sqrt(HEAD_DIM)
        where = lax.broadcasted_iota(jnp.int32, scores.shape, 1)
        scores = jnp.where(where < lives[k], scores, -jnp.inf)
        top = jnp.max(scores, axis=-1, keepdims=True)
        lifted = jnp.exp(scores - top)
        total = jnp.sum(lifted, axis=-1, keepdims=True)
        mixed = (
            jnp.dot(lifted.astype(jnp.bfloat16), values, preferred_element_type=jnp.float32)
            / total
        ).astype(jnp.bfloat16)
        start = pl.multiple_of(group * rows, rows)
        for h in range(heads):
            attended[pl.ds(start, rows), h * HEAD_DIM : (h + 1) * HEAD_DIM] = mixed[
                h * rows : (h + 1) * rows, :
            ]
    product = jnp.dot(attended[...], w_ref[...], preferred_element_type=jnp.float32)
    for g in range(attn):
        for s in range(sect):
            for p in range(pair):
                source = g * rows + (s * pair + p) * per_dev
                target = (s * attn + g) * per_dev
                split[p, target : target + per_dev, :] = product[source : source + per_dev, :]
    for k in range(attn):
        group = lax.rem(me + attn - k, attn)
        target = pl.ds(pl.multiple_of((my_sect * attn + group) * per_dev, per_dev), per_dev)
        block = pack_refs[k][low : low + per_dev, :]
        split[my_pair, target, :] += block[:, :width].astype(jnp.float32)
        lanes = pl.ds(pl.multiple_of(group * 128, 128), 128)
        ids_ref[:, lanes] = block[:, width : width + 128]
    for i in range(pair):
        part_refs[i][...] = split[lax.rem(my_pair + i, pair)]


def pair_sum_kernel(pair, kept_ref, *refs):
    came, (ids_ref, total_ref, sent_ref) = refs[: pair - 1], refs[pair - 1 :]
    total = kept_ref[...]
    for ref in came:
        total = total + ref[...]
    total_ref[...] = total
    rows = total.shape[0]
    sent_ref[:rows, :] = total.astype(jnp.bfloat16)
    sent_ref[rows:, : ids_ref.shape[1]] = ids_ref[...]
    if ids_ref.shape[1] < total.shape[1]:
        sent_ref[rows:, ids_ref.shape[1] :] = jnp.zeros(
            (ids_ref.shape[0], total.shape[1] - ids_ref.shape[1]), jnp.bfloat16
        )


def sect_sum_kernel(sect, kept_ref, own_ref, *refs):
    came, (mixed_ref, sent_ref) = refs[: sect - 1], refs[sect - 1 :]
    my_sect = lax.axis_index("sect")
    total = kept_ref[...]
    rows = total.shape[0]
    per_dev = own_ref.shape[0] - rows
    for ref in came:
        total = total + ref[:rows, :].astype(jnp.float32)
    mixed = total.astype(jnp.bfloat16)
    mixed_ref[...] = mixed
    sent_ref[:rows, :] = mixed
    for i, ref in enumerate((own_ref,) + tuple(came)):
        from_sect = lax.rem(my_sect + sect - i, sect)
        place = pl.ds(pl.multiple_of(rows + from_sect * per_dev, per_dev), per_dev)
        sent_ref[place, :] = ref[rows:, :]


def expert_kernel(attn, sect, pair, per_dev, top, *refs):
    piece_refs, refs = refs[: attn * pair], refs[attn * pair :]
    gain_ref, router_ref, gate_ref, up_ref, refs = *refs[:4], refs[4:]
    down_refs, refs = refs[:sect], refs[sect:]
    part_refs, refs = refs[:pair], refs[pair:]
    own_ref, ids_all, contribution = refs
    half = attn * sect * per_dev
    width = piece_refs[0].shape[1]
    model = width * attn
    me, my_sect, my_pair = (lax.axis_index(n) for n in ("attn", "sect", "pair"))
    my_expert = me * pair + my_pair
    rows = half * pair
    values = []
    squares = jnp.zeros((rows, 1), jnp.float32)
    for k in range(attn):
        value = jnp.concatenate(
            [piece_refs[j * attn + k][:half, :] for j in range(pair)], axis=0
        ).astype(jnp.float32)
        values.append(value)
        squares = squares + jnp.sum(value * value, axis=-1, keepdims=True)
    scale = lax.rsqrt(squares / model + 1e-06)
    gate = up = logits = None
    own_start = pl.multiple_of((my_sect * attn + me) * per_dev, per_dev)
    for k in range(attn):
        group = lax.rem(me + attn - k, attn)
        cols = pl.ds(pl.multiple_of(group * width, width), width)
        lines = width // 128
        gain = jnp.concatenate(
            [gain_ref[pl.ds(group * lines + j, 1), :] for j in range(lines)], axis=1
        )
        normed = (values[k] * scale * gain).astype(jnp.bfloat16)
        parts = [
            jnp.dot(normed, ref[cols, :], preferred_element_type=jnp.float32)
            for ref in (gate_ref, up_ref)
        ] + [
            lax.dot_general(
                normed,
                router_ref[:, cols],
                (((1,), (1,)), ((), ())),
                preferred_element_type=jnp.float32,
            )
        ]
        if k == 0:
            gate, up, logits = parts
        else:
            gate, up, logits = gate + parts[0], up + parts[1], logits + parts[2]
        own_ref[:, cols] = piece_refs[k][pl.ds(own_start, per_dev), :]
    for j in range(pair):
        for s in range(sect):
            block = piece_refs[j * attn][half + s * per_dev : half + (s + 1) * per_dev, :]
            block = block.astype(jnp.float32)
            for g in range(attn):
                target = j * half + (s * attn + g) * per_dev
                ids_all[target : target + per_dev, :] = block[:, g * 128 : g * 128 + top]
    ids = ids_all[...]
    lane = lax.broadcasted_iota(jnp.int32, logits.shape, 1)
    lane_f = lane.astype(jnp.float32)
    named = lane < 0
    for c in range(top):
        named = named | (ids[:, c : c + 1] == lane_f)
    chosen = jnp.where(named, logits, -jnp.inf)
    lifted = jnp.exp(chosen - jnp.max(chosen, axis=-1, keepdims=True))
    weights = lifted / jnp.sum(lifted, axis=-1, keepdims=True)
    weight = jnp.sum(jnp.where(lane == my_expert, weights, 0.0), axis=-1, keepdims=True)
    hidden = (gate / (1.0 + jnp.exp(-gate)) * up).astype(jnp.bfloat16)
    section = down_refs[0].shape[1]
    for i in range(sect):
        from_sect = lax.rem(my_sect + sect - i, sect)
        cols = pl.ds(pl.multiple_of(from_sect * section, section), section)
        contribution[:, cols] = (
            jnp.dot(hidden, down_refs[i][...], preferred_element_type=jnp.float32) * weight
        )
    part_refs[0][...] = contribution[:half, :]
    for j in range(1, pair):
        part_refs[j][...] = contribution[j * half : (j + 1) * half, :].astype(jnp.bfloat16)


def split_kernel(axis, size, count, kept_ref, *refs):
    came, outs = refs[:count], refs[count:]
    me = lax.axis_index(axis)
    part = kept_ref.shape[0] // size
    for i in range(size):
        rows = pl.ds(pl.multiple_of(lax.rem(me + i, size) * part, part), part)
        total = kept_ref[rows, :]
        for ref in came:
            total = total + ref[rows, :].astype(jnp.float32)
        outs[i][...] = total.astype(outs[i].dtype)


def call(kernel, operands, outs, scratch=(), limit=4 << 20, flops=1 << 20):
    moved = sum(x.size * x.dtype.itemsize for x in operands)
    return pl.pallas_call(
        kernel,
        out_shape=outs,
        in_specs=[VMEM] * len(operands),
        out_specs=jax.tree.map(lambda _: VMEM, outs),
        scratch_shapes=list(scratch),
        compiler_params=pltpu.CompilerParams(vmem_limit_bytes=limit),
        cost_estimate=pl.CostEstimate(flops=flops, bytes_accessed=moved, transcendentals=0),
    )(*operands)


def dense_layer(
    queries,
    kv_pool,
    block_list,
    cache_len,
    out_weight,
    residual,
    norm_gain,
    router,
    expert_ids,
    w_gate,
    w_up,
    w_down,
):
    attn, sect, pair = (lax.axis_size(n) for n in ("attn", "sect", "pair"))
    bf16, f32 = jnp.bfloat16, jnp.float32
    shape = jax.ShapeDtypeStruct
    rows, head_cols = queries.shape
    per_dev, model = residual.shape
    top = expert_ids.shape[1]
    width = out_weight.shape[1]
    ff = w_gate.shape[2]
    list_len = block_list.shape[1]
    _, blocks, keys, kv_cols = kv_pool.shape
    folds = head_cols // kv_cols
    half = attn * sect * per_dev
    low = blocks * keys // folds

    q = {0: queries}
    for k in steps_of(attn):
        q[k] = rotate(queries, "attn", k)
    outs = call(
        functools.partial(pack_kernel, attn),
        [kv_pool, block_list, cache_len.reshape(1, 1), residual, expert_ids.T],
        [shape((low + per_dev, head_cols), bf16)] * attn,
    )
    packs = {0: outs[0]}
    for k in steps_of(attn):
        packs[k] = rotate(outs[k], "attn", k)
    downs = call(
        functools.partial(halves_kernel, sect),
        [w_down[0]],
        [shape((ff, w_down.shape[2]), bf16)] * sect,
    )
    downs = [downs[0]] + [rotate(downs[i], "sect", i) for i in range(1, sect)]

    parts = call(
        functools.partial(
            attend_kernel, attn, sect, pair, list_len, rows, blocks, keys, kv_cols
        ),
        [q[k] for k in range(attn)] + [packs[k] for k in range(attn)] + [out_weight],
        [shape((half, width), f32)] * pair + [shape((per_dev, attn * 128), bf16)],
        [
            pltpu.VMEM((attn * blocks, keys, kv_cols), bf16),
            pltpu.VMEM((attn * rows, head_cols), bf16),
            pltpu.VMEM((pair, half, width), f32),
        ],
        limit=16 << 20,
    )
    total, sent = call(
        functools.partial(pair_sum_kernel, pair),
        [parts[0]] + [rotate(parts[j], "pair", j) for j in range(1, pair)] + [parts[pair]],
        [shape((half, width), f32), shape((half + per_dev, width), bf16)],
    )
    mixed, named = call(
        functools.partial(sect_sum_kernel, sect),
        [total, sent] + [rotate(sent, "sect", i) for i in range(1, sect)],
        [shape((half, width), bf16), shape((half + sect * per_dev, width), bf16)],
    )
    piece = {0: named}
    for k in steps_of(attn):
        piece[k] = rotate(mixed, "attn", k)
    pieces = [piece[k] for k in range(attn)]
    for j in range(1, pair):
        pieces += [rotate(piece[k], "pair", j) for k in range(attn)]

    outs = call(
        functools.partial(expert_kernel, attn, sect, pair, per_dev, top),
        pieces
        + [norm_gain.reshape(-1, 128), router.T, w_gate[0], w_up[0]]
        + downs,
        [shape((half, model), f32)]
        + [shape((half, model), bf16)] * (pair - 1)
        + [shape((per_dev, model), bf16)],
        [
            pltpu.VMEM((half * pair, top), f32),
            pltpu.VMEM((half * pair, model), f32),
        ],
        limit=24 << 20,
    )
    own_mixed = outs[pair]
    came = [rotate(outs[j], "pair", pair - j) for j in range(1, pair)]
    part = half // sect
    outs = call(
        functools.partial(split_kernel, "sect", sect, pair - 1),
        [outs[0]] + came,
        [shape((part, model), f32)] + [shape((part, model), bf16)] * (sect - 1),
    )
    came = [rotate(outs[i], "sect", i) for i in range(1, sect)]
    outs = call(
        functools.partial(split_kernel, "attn", attn, sect - 1),
        [outs[0]] + came,
        [shape((per_dev, model), f32)] + [shape((per_dev, model), bf16)] * (attn - 1),
    )
    total = own_mixed.astype(f32) + outs[0]
    for k in steps_of(attn):
        total = total + rotate(outs[k], "attn", k).astype(f32)
    return total.astype(bf16)


def on_device(*operands):
    queries, expert_ids, router = operands[0], operands[8], operands[7]
    row_count, top_count = expert_ids.shape
    capacity = max(2, row_count * top_count // router.shape[1] * 2)
    local_heads = queries.shape[1] // HEAD_DIM
    one_each = operands[9].shape[0] == 1
    if capacity >= row_count and one_each and local_heads <= HEADS // KV_HEADS:
        return dense_layer(*operands)
    return routed_layer(*operands)


def solution(mesh):
    placed = (
        P(("group", "attn"), ("sect", "pair")),
        P("sect", ("group", "attn"), None, None),
        P(("group", "attn"), None),
        P(("group", "attn")),
        P(("sect", "pair"), "attn"),
        P(("group", "attn", "sect", "pair"), None),
        P(),
        P(),
        P(("group", "attn", "sect", "pair"), None),
        P(("attn", "pair"), None, "sect"),
        P(("attn", "pair"), None, "sect"),
        P(("attn", "pair"), None, "sect"),
    )
    return jax.shard_map(
        on_device,
        mesh=mesh,
        in_specs=placed,
        out_specs=P(("group", "attn", "sect", "pair"), None),
        check_vma=False,
    )
```

```python
import functools
import math

import jax
import jax.numpy as jnp
from jax import lax
from jax.experimental import pallas as pl
from jax.experimental.pallas import tpu as pltpu
from jax.sharding import PartitionSpec as P


HEADS = 32
KV_HEADS = 4
HEAD_DIM = 128


VMEM = pl.BlockSpec(memory_space=pltpu.VMEM)


def routed_layer(
    queries,
    kv_pool,
    block_list,
    cache_len,
    out_weight,
    residual,
    norm_gain,
    router,
    expert_ids,
    w_gate,
    w_up,
    w_down,
):
    head_dim = HEAD_DIM
    per_kv = HEADS // KV_HEADS
    group_rows, head_cols = queries.shape
    local_heads = head_cols // head_dim
    pool_all = lax.all_gather(kv_pool, "attn", axis=1, tiled=True)
    picked = jnp.take(pool_all, block_list[0], axis=1)
    kv_local = lax.axis_index("pair") * local_heads // per_kv
    chosen = lax.dynamic_index_in_dim(picked, kv_local, 0, keepdims=False)
    chosen = chosen.reshape(-1, 2 * head_dim)
    key_rows = chosen[:, :head_dim]
    values = chosen[:, head_dim:]
    query_heads = queries.reshape(group_rows, local_heads, head_dim)
    scores = jnp.einsum(
        "rhd,td->rht", query_heads, key_rows, preferred_element_type=jnp.float32
    ) / math.sqrt(head_dim)
    live_mask = jnp.arange(key_rows.shape[0]) < cache_len[0]
    scores = jnp.where(live_mask, scores, -jnp.inf)
    row_top = jnp.max(scores, axis=-1, keepdims=True)
    lifted = jnp.exp(scores - row_top)
    row_total = jnp.sum(lifted, axis=-1)
    soft_weights = lifted.astype(jnp.bfloat16)
    mixed_heads = (
        jnp.einsum("rht,td->rhd", soft_weights, values, preferred_element_type=jnp.float32)
        / row_total[..., None]
    )
    attended = mixed_heads.reshape(group_rows, head_cols).astype(jnp.bfloat16)
    partial_value = jnp.dot(
        attended,
        lax.all_gather(out_weight, "attn", axis=1, tiled=True),
        preferred_element_type=jnp.float32,
    )
    summed = lax.psum_scatter(partial_value, ("sect", "pair"), scatter_dimension=0, tiled=True)
    mixed_f32 = residual.astype(jnp.float32) + summed
    mixed_rows = mixed_f32.astype(jnp.bfloat16)
    mixed_f32 = mixed_rows.astype(jnp.float32)
    normed = (
        mixed_f32
        * lax.rsqrt(jnp.mean(mixed_f32 * mixed_f32, axis=-1, keepdims=True) + 1e-06)
        * norm_gain
    ).astype(jnp.bfloat16)
    logits = jnp.dot(normed, router, preferred_element_type=jnp.float32)
    chosen_logits = jnp.take_along_axis(logits, expert_ids, axis=1)
    route_weights = jax.nn.softmax(chosen_logits, axis=-1)
    row_count, top_count = expert_ids.shape
    expert_count = router.shape[1]
    model_width = residual.shape[1]
    capacity = max(2, row_count * top_count // expert_count * 2)
    flat_ids = expert_ids.reshape(-1)
    onehot = (flat_ids[:, None] == jnp.arange(expert_count, dtype=jnp.int32)[None, :]).astype(
        jnp.int32
    )
    earlier = jnp.cumsum(onehot, axis=0) - onehot
    slot_index = jnp.sum(earlier * onehot, axis=1)
    source = jnp.repeat(jnp.arange(row_count, dtype=jnp.int32), top_count)
    outgoing = (
        jnp.zeros((expert_count, capacity, model_width), jnp.bfloat16)
        .at[flat_ids, slot_index]
        .set(normed[source])
    )
    received = lax.all_to_all(outgoing, ("attn", "pair"), split_axis=0, concat_axis=0, tiled=True)
    sections = lax.axis_size("sect")
    every_section = lax.all_gather(received, "sect", axis=0, tiled=True)
    tokens_in = every_section.reshape(-1, model_width)
    gate_val = jnp.dot(tokens_in, w_gate[0], preferred_element_type=jnp.float32)
    up_val = jnp.dot(tokens_in, w_up[0], preferred_element_type=jnp.float32)
    part_hidden = (jax.nn.silu(gate_val) * up_val).astype(jnp.bfloat16)
    hidden = lax.all_gather(part_hidden, "sect", axis=1, tiled=True)
    out_slice = jnp.dot(hidden, w_down[0], preferred_element_type=jnp.float32).astype(jnp.bfloat16)
    out_slice = out_slice.reshape(sections, expert_count, capacity, model_width // sections)
    segmented = lax.all_to_all(out_slice, "sect", split_axis=0, concat_axis=3, tiled=True)
    returned = lax.all_to_all(
        segmented[0], ("attn", "pair"), split_axis=0, concat_axis=0, tiled=True
    )
    gathered = (
        returned[flat_ids, slot_index]
        .reshape(row_count, top_count, model_width)
        .astype(jnp.float32)
    )
    joined = jnp.sum(route_weights[:, :, None] * gathered, axis=1)
    return (mixed_f32 + joined).astype(jnp.bfloat16)


def rotate(value, axis, step):
    size = lax.axis_size(axis)
    return lax.ppermute(value, axis, [(i, (i + step) % size) for i in range(size)])


def swap(value, axis, mask):
    size = lax.axis_size(axis)
    return lax.ppermute(value, axis, [(i, i ^ mask) for i in range(size)])


def anchor_kernel(out_ref):
    out_ref[...] = jnp.zeros_like(out_ref)


def pack_kernel(attn, sect, *refs):
    _, q_ref, kv_ref, list_ref, len_ref, res_ref, ids_ref, down_ref, *refs = refs
    own_ref, far_ref, near_ref, q_out, *downs = refs
    my_attn, my_sect = lax.axis_index("attn"), lax.axis_index("sect")
    q_out[...] = q_ref[...]
    ff = downs[0].shape[0]
    for i in range(sect):
        start = pl.multiple_of(lax.rem(my_sect + i, sect) * ff, ff)
        downs[i][...] = down_ref[pl.ds(start, ff), :]
    per_dev = res_ref.shape[0]
    top = ids_ref.shape[0]
    width = res_ref.shape[1] // attn
    _, blocks, keys, kv_cols = kv_ref.shape
    folds = width // kv_cols
    local_heads = HEADS // (lax.axis_size("sect") * lax.axis_size("pair"))
    kv_local = lax.axis_index("pair") * local_heads // (HEADS // KV_HEADS)
    lane = lax.broadcasted_iota(jnp.int32, (per_dev, kv_cols - 128), 1)
    facts = jnp.zeros((per_dev, kv_cols - 128), jnp.int32)
    list_len = list_ref.shape[1]
    for j in range(list_len):
        facts = jnp.where(lane == j, list_ref[:, j : j + 1], facts)
    facts = jnp.where(lane == list_len, len_ref[...] // 128, facts)
    facts = jnp.where(lane == list_len + 1, lax.rem(len_ref[...], 128), facts)
    facts = facts.astype(jnp.float32).astype(jnp.bfloat16)
    eye = (
        lax.broadcasted_iota(jnp.int32, (per_dev, per_dev), 0)
        == lax.broadcasted_iota(jnp.int32, (per_dev, per_dev), 1)
    )
    ids = lax.dot_general(
        eye.astype(jnp.float32).astype(jnp.bfloat16),
        ids_ref[...].astype(jnp.float32).astype(jnp.bfloat16),
        (((1,), (1,)), ((), ())),
        preferred_element_type=jnp.float32,
    )
    ids = jnp.concatenate([ids, jnp.zeros((per_dev, 128 - top), jnp.float32)], axis=1)
    named = jnp.concatenate([ids.astype(jnp.bfloat16), facts], axis=1)

    def put_slice(ref, row, receiver):
        for f in range(folds):
            start = pl.multiple_of(receiver * width + f * kv_cols, kv_cols)
            ref[row + f * per_dev : row + (f + 1) * per_dev, :] = res_ref[:, pl.ds(start, kv_cols)]

    first = folds * per_dev
    after = first + blocks * keys
    for ref, mask in ((own_ref, 0), (far_ref, 2), (near_ref, 1)):
        put_slice(ref, 0, my_attn ^ mask)
        for b in range(blocks):
            ref[first + b * keys : first + (b + 1) * keys, :] = kv_ref[kv_local, b]
        ref[after : after + per_dev, :] = named
    put_slice(far_ref, after + per_dev, my_attn ^ 3)


def attend_kernel(attn, sect, pair, list_len, blocks, keys, *refs):
    q_refs, refs = refs[:attn], refs[attn:]
    pack_refs, refs = refs[:attn], refs[attn:]
    w_ref, refs = refs[0], refs[1:]
    part_refs, refs = refs[:pair], refs[pair:]
    ids_ref, pool, attended, split = refs
    per_dev = ids_ref.shape[0]
    rows, head_cols = q_refs[0].shape
    kv_cols = pack_refs[0].shape[1]
    width = w_ref.shape[1]
    heads = head_cols // HEAD_DIM
    folds = width // kv_cols
    me, my_sect, my_pair = (lax.axis_index(n) for n in ("attn", "sect", "pair"))
    lane = lax.broadcasted_iota(jnp.int32, (1, kv_cols - 128), 1)
    cache_at = [0 if k == 3 else folds * per_dev for k in range(attn)]
    named_at = [at + blocks * keys for at in cache_at]
    slice_at = [named_at[k] + per_dev if k == 3 else 0 for k in range(attn)]
    lists, lives = [], []
    for k in range(attn):
        group = me ^ k
        for b in range(blocks):
            at = cache_at[k] + b * keys
            pool[group * blocks + b] = pack_refs[k][at : at + keys, :]
        facts = pack_refs[k][named_at[k] : named_at[k] + per_dev, 128:]
        facts = facts.astype(jnp.float32)[0:1, :]

        def fact(j, facts=facts):
            return jnp.sum(jnp.where(lane == j, facts, 0.0)).astype(jnp.int32)

        lists.append([fact(j) for j in range(list_len)])
        lives.append(fact(list_len) * 128 + fact(list_len + 1))
    for k in range(attn):
        group = me ^ k
        picked = [pool[index] for index in lists[k]]
        key_rows = jnp.concatenate([p[:, :HEAD_DIM] for p in picked], axis=0)
        values = jnp.concatenate([p[:, HEAD_DIM:] for p in picked], axis=0)
        q_all = q_refs[k][...]
        stacked = jnp.concatenate(
            [q_all[:, h * HEAD_DIM : (h + 1) * HEAD_DIM] for h in range(heads)], axis=0
        )
        scores = lax.dot_general(
            stacked, key_rows, (((1,), (1,)), ((), ())), preferred_element_type=jnp.float32
        ) / math.sqrt(HEAD_DIM)
        where = lax.broadcasted_iota(jnp.int32, scores.shape, 1)
        scores = jnp.where(where < lives[k], scores, -jnp.inf)
        top = jnp.max(scores, axis=-1, keepdims=True)
        lifted = jnp.exp(scores - top)
        total = jnp.sum(lifted, axis=-1, keepdims=True)
        mixed = (
            jnp.dot(lifted.astype(jnp.bfloat16), values, preferred_element_type=jnp.float32)
            / total
        ).astype(jnp.bfloat16)
        start = pl.multiple_of(group * rows, rows)
        for h in range(heads):
            attended[pl.ds(start, rows), h * HEAD_DIM : (h + 1) * HEAD_DIM] = mixed[
                h * rows : (h + 1) * rows, :
            ]
    product = jnp.dot(attended[...], w_ref[...], preferred_element_type=jnp.float32)
    for g in range(attn):
        for s in range(sect):
            for p in range(pair):
                source = g * rows + (s * pair + p) * per_dev
                target = (s * attn + g) * per_dev
                split[p, target : target + per_dev, :] = product[source : source + per_dev, :]
    for k in range(attn):
        group = me ^ k
        target = pl.ds(pl.multiple_of((my_sect * attn + group) * per_dev, per_dev), per_dev)
        for f in range(folds):
            at = slice_at[k] + f * per_dev
            split[my_pair, target, f * kv_cols : (f + 1) * kv_cols] += pack_refs[k][
                at : at + per_dev, :
            ].astype(jnp.float32)
        lanes = pl.ds(pl.multiple_of(group * 128, 128), 128)
        ids_ref[:, lanes] = pack_refs[k][named_at[k] : named_at[k] + per_dev, :128]
    for i in range(pair):
        part_refs[i][...] = split[lax.rem(my_pair + i, pair)]


def pair_sum_kernel(pair, kept_ref, *refs):
    came, (ids_ref, total_ref, sent_ref) = refs[: pair - 1], refs[pair - 1 :]
    total = kept_ref[...]
    for ref in came:
        total = total + ref[...]
    total_ref[...] = total
    rows = total.shape[0]
    sent_ref[:rows, :] = total.astype(jnp.bfloat16)
    sent_ref[rows:, : ids_ref.shape[1]] = ids_ref[...]
    if ids_ref.shape[1] < total.shape[1]:
        sent_ref[rows:, ids_ref.shape[1] :] = jnp.zeros(
            (ids_ref.shape[0], total.shape[1] - ids_ref.shape[1]), jnp.bfloat16
        )


def sect_sum_kernel(sect, kept_ref, own_ref, *refs):
    came, (mixed_ref, sent_ref) = refs[: sect - 1], refs[sect - 1 :]
    my_sect = lax.axis_index("sect")
    total = kept_ref[...]
    rows = total.shape[0]
    per_dev = own_ref.shape[0] - rows
    for ref in came:
        total = total + ref[:rows, :].astype(jnp.float32)
    mixed = total.astype(jnp.bfloat16)
    mixed_ref[...] = mixed
    sent_ref[:rows, :] = mixed
    for i, ref in enumerate((own_ref,) + tuple(came)):
        from_sect = lax.rem(my_sect + sect - i, sect)
        place = pl.ds(pl.multiple_of(rows + from_sect * per_dev, per_dev), per_dev)
        sent_ref[place, :] = ref[rows:, :]


def expert_kernel(attn, sect, pair, per_dev, top, shift, *refs):
    piece_refs, refs = refs[: attn * pair], refs[attn * pair :]
    gain_ref, router_ref, gate_ref, up_ref, refs = *refs[:4], refs[4:]
    down_refs, refs = refs[:sect], refs[sect:]
    part_refs, refs = refs[:pair], refs[pair:]
    own_refs, (ids_all, contribution) = refs[:-2], refs[-2:]
    part = attn * per_dev
    half = part * sect
    width = piece_refs[0].shape[1]
    model = width * attn
    me, my_sect, my_pair = (lax.axis_index(n) for n in ("attn", "sect", "pair"))
    my_expert = me * pair + my_pair
    section = lax.rem(my_sect + shift, sect)
    block_rows = pl.ds(pl.multiple_of(section * part, part), part)
    rows = part * pair
    values = []
    squares = jnp.zeros((rows, 1), jnp.float32)
    for k in range(attn):
        value = jnp.concatenate(
            [piece_refs[j * attn + k][block_rows, :] for j in range(pair)], axis=0
        ).astype(jnp.float32)
        values.append(value)
        squares = squares + jnp.sum(value * value, axis=-1, keepdims=True)
    scale = lax.rsqrt(squares / model + 1e-06)
    gate = up = logits = None
    own_start = pl.multiple_of((my_sect * attn + me) * per_dev, per_dev)
    for k in range(attn):
        group = me ^ k
        cols = pl.ds(pl.multiple_of(group * width, width), width)
        lines = width // 128
        gain = jnp.concatenate(
            [gain_ref[pl.ds(group * lines + j, 1), :] for j in range(lines)], axis=1
        )
        normed = (values[k] * scale * gain).astype(jnp.bfloat16)
        parts = [
            jnp.dot(normed, ref[cols, :], preferred_element_type=jnp.float32)
            for ref in (gate_ref, up_ref)
        ] + [
            lax.dot_general(
                normed,
                router_ref[:, cols],
                (((1,), (1,)), ((), ())),
                preferred_element_type=jnp.float32,
            )
        ]
        if k == 0:
            gate, up, logits = parts
        else:
            gate, up, logits = gate + parts[0], up + parts[1], logits + parts[2]
        for own_ref in own_refs:
            own_ref[:, cols] = piece_refs[k][pl.ds(own_start, per_dev), :]
    for j in range(pair):
        names = pl.ds(pl.multiple_of(half + section * per_dev, per_dev), per_dev)
        block = piece_refs[j * attn][names, :].astype(jnp.float32)
        for g in range(attn):
            target = j * part + g * per_dev
            ids_all[target : target + per_dev, :] = block[:, g * 128 : g * 128 + top]
    ids = ids_all[...]
    lane = lax.broadcasted_iota(jnp.int32, logits.shape, 1)
    lane_f = lane.astype(jnp.float32)
    named = lane < 0
    for c in range(top):
        named = named | (ids[:, c : c + 1] == lane_f)
    chosen = jnp.where(named, logits, -jnp.inf)
    lifted = jnp.exp(chosen - jnp.max(chosen, axis=-1, keepdims=True))
    weights = lifted / jnp.sum(lifted, axis=-1, keepdims=True)
    weight = jnp.sum(jnp.where(lane == my_expert, weights, 0.0), axis=-1, keepdims=True)
    hidden = (gate / (1.0 + jnp.exp(-gate)) * up).astype(jnp.bfloat16)
    columns = down_refs[0].shape[1]
    for i in range(sect):
        from_sect = lax.rem(my_sect + sect - i, sect)
        cols = pl.ds(pl.multiple_of(from_sect * columns, columns), columns)
        contribution[:, cols] = (
            jnp.dot(hidden, down_refs[i][...], preferred_element_type=jnp.float32) * weight
        )
    part_refs[0][...] = contribution[:part, :]
    for j in range(1, pair):
        part_refs[j][...] = contribution[j * part : (j + 1) * part, :].astype(jnp.bfloat16)


def sum_kernel(kept_ref, *refs):
    *came, out_ref = refs
    total = kept_ref[...]
    for ref in came:
        total = total + ref[...].astype(jnp.float32)
    out_ref[...] = total.astype(out_ref.dtype)


def split_kernel(attn, kept_ref, *refs):
    came, outs = refs[:-attn], refs[-attn:]
    me = lax.axis_index("attn")
    part = kept_ref.shape[0] // attn
    for i in range(attn):
        rows = pl.ds(pl.multiple_of((me ^ i) * part, part), part)
        total = kept_ref[rows, :]
        for ref in came:
            total = total + ref[rows, :].astype(jnp.float32)
        outs[i][...] = total.astype(outs[i].dtype)


def call(kernel, operands, outs, scratch=(), limit=4 << 20, flops=1 << 20):
    moved = sum(x.size * x.dtype.itemsize for x in operands)
    return pl.pallas_call(
        kernel,
        out_shape=outs,
        in_specs=[VMEM] * len(operands),
        out_specs=jax.tree.map(lambda _: VMEM, outs),
        scratch_shapes=list(scratch),
        compiler_params=pltpu.CompilerParams(vmem_limit_bytes=limit),
        cost_estimate=pl.CostEstimate(flops=flops, bytes_accessed=moved, transcendentals=0),
    )(*operands)


def dense_layer(
    queries,
    kv_pool,
    block_list,
    cache_len,
    out_weight,
    residual,
    norm_gain,
    router,
    expert_ids,
    w_gate,
    w_up,
    w_down,
):
    attn, sect, pair = (lax.axis_size(n) for n in ("attn", "sect", "pair"))
    bf16, f32 = jnp.bfloat16, jnp.float32
    shape = jax.ShapeDtypeStruct
    rows, head_cols = queries.shape
    per_dev, model = residual.shape
    top = expert_ids.shape[1]
    width = out_weight.shape[1]
    ff = w_gate.shape[2]
    list_len = block_list.shape[1]
    _, blocks, keys, kv_cols = kv_pool.shape
    half = attn * sect * per_dev
    slice_rows = per_dev * width // kv_cols
    packed = slice_rows + blocks * keys + per_dev

    anchor = call(anchor_kernel, [], shape((8, 128), f32), flops=1 << 34)
    own_pack, far_pack, near_pack, own_q, *downs = call(
        functools.partial(pack_kernel, attn, sect),
        [
            anchor,
            queries,
            kv_pool,
            block_list,
            cache_len.reshape(1, 1),
            residual,
            expert_ids.T,
            w_down[0],
        ],
        [
            shape((packed, kv_cols), bf16),
            shape((packed + slice_rows, kv_cols), bf16),
            shape((packed, kv_cols), bf16),
            shape(queries.shape, bf16),
        ]
        + [shape((ff, w_down.shape[2]), bf16)] * sect,
    )
    far_pack = swap(far_pack, "attn", 2)
    far_q = swap(own_q, "attn", 2)
    downs = [downs[0]] + [rotate(downs[i], "sect", i) for i in range(1, sect)]
    near_pack = swap(near_pack, "attn", 1)
    near_q = swap(own_q, "attn", 1)
    last_pack = swap(far_pack[slice_rows:], "attn", 1)
    last_q = swap(far_q, "attn", 1)
    q = [own_q, near_q, far_q, last_q]
    packs = [own_pack, near_pack, far_pack, last_pack]

    parts = call(
        functools.partial(
            attend_kernel, attn, sect, pair, list_len, blocks, keys
        ),
        q + packs + [out_weight],
        [shape((half, width), f32)] * pair + [shape((per_dev, attn * 128), bf16)],
        [
            pltpu.VMEM((attn * blocks, keys, kv_cols), bf16),
            pltpu.VMEM((attn * rows, head_cols), bf16),
            pltpu.VMEM((pair, half, width), f32),
        ],
        limit=16 << 20,
    )
    total, sent = call(
        functools.partial(pair_sum_kernel, pair),
        [parts[0]] + [rotate(parts[j], "pair", j) for j in range(1, pair)] + [parts[pair]],
        [shape((half, width), f32), shape((half + per_dev, width), bf16)],
    )
    mixed, named = call(
        functools.partial(sect_sum_kernel, sect),
        [total, sent] + [rotate(sent, "sect", i) for i in range(1, sect)],
        [shape((half, width), bf16), shape((half + sect * per_dev, width), bf16)],
    )
    piece = {0: named}
    for k in range(1, attn):
        piece[k] = swap(mixed, "attn", k)
    pieces = [piece[k] for k in range(attn)]
    for j in range(1, pair):
        pieces += [rotate(piece[k], "pair", j) for k in range(attn)]

    operands = pieces + [norm_gain.reshape(-1, 128), router.T, w_gate[0], w_up[0]] + downs
    part = attn * per_dev

    def experts(shift):
        outs = call(
            functools.partial(expert_kernel, attn, sect, pair, per_dev, top, shift),
            operands,
            [shape((part, model), f32)]
            + [shape((part, model), bf16)] * (pair - 1)
            + [shape((per_dev, model), bf16)] * (shift == 0),
            [pltpu.VMEM((part * pair, top), f32), pltpu.VMEM((part * pair, model), f32)],
            limit=16 << 20,
            flops=1 << 31,
        )
        came = [rotate(outs[j], "pair", pair - j) for j in range(1, pair)]
        return outs, came

    from_sect = []
    for i in range(1, sect):
        outs, came = experts(i)
        sent = call(sum_kernel, [outs[0]] + came, shape((part, model), bf16))
        from_sect.append(rotate(sent, "sect", i))
    outs, came = experts(0)
    own_mixed = outs[pair]
    outs = call(
        functools.partial(split_kernel, attn),
        [outs[0]] + came + from_sect,
        [shape((per_dev, model), f32)] + [shape((per_dev, model), bf16)] * (attn - 1),
    )
    total = own_mixed.astype(f32) + outs[0]
    for k in range(1, attn):
        total = total + swap(outs[k], "attn", k).astype(f32)
    return total.astype(bf16)


def on_device(*operands):
    queries, expert_ids, router = operands[0], operands[8], operands[7]
    row_count, top_count = expert_ids.shape
    capacity = max(2, row_count * top_count // router.shape[1] * 2)
    local_heads = queries.shape[1] // HEAD_DIM
    one_each = operands[9].shape[0] == 1 and lax.axis_size("attn") == 4
    if capacity >= row_count and one_each and local_heads <= HEADS // KV_HEADS:
        return dense_layer(*operands)
    return routed_layer(*operands)


def solution(mesh):
    placed = (
        P(("group", "attn"), ("sect", "pair")),
        P("sect", ("group", "attn"), None, None),
        P(("group", "attn"), None),
        P(("group", "attn")),
        P(("sect", "pair"), "attn"),
        P(("group", "attn", "sect", "pair"), None),
        P(),
        P(),
        P(("group", "attn", "sect", "pair"), None),
        P(("attn", "pair"), None, "sect"),
        P(("attn", "pair"), None, "sect"),
        P(("attn", "pair"), None, "sect"),
    )
    return jax.shard_map(
        on_device,
        mesh=mesh,
        in_specs=placed,
        out_specs=P(("group", "attn", "sect", "pair"), None),
        check_vma=False,
    )
```

```python
import functools
import math

import jax
import jax.numpy as jnp
from jax import lax
from jax.experimental import pallas as pl
from jax.experimental.pallas import tpu as pltpu
from jax.sharding import PartitionSpec as P


HEADS = 32
KV_HEADS = 4
HEAD_DIM = 128


VMEM = pl.BlockSpec(memory_space=pltpu.VMEM)


def routed_layer(
    queries,
    kv_pool,
    block_list,
    cache_len,
    out_weight,
    residual,
    norm_gain,
    router,
    expert_ids,
    w_gate,
    w_up,
    w_down,
):
    head_dim = HEAD_DIM
    per_kv = HEADS // KV_HEADS
    group_rows, head_cols = queries.shape
    local_heads = head_cols // head_dim
    pool_all = lax.all_gather(kv_pool, "attn", axis=1, tiled=True)
    picked = jnp.take(pool_all, block_list[0], axis=1)
    kv_local = lax.axis_index("pair") * local_heads // per_kv
    chosen = lax.dynamic_index_in_dim(picked, kv_local, 0, keepdims=False)
    chosen = chosen.reshape(-1, 2 * head_dim)
    key_rows = chosen[:, :head_dim]
    values = chosen[:, head_dim:]
    query_heads = queries.reshape(group_rows, local_heads, head_dim)
    scores = jnp.einsum(
        "rhd,td->rht", query_heads, key_rows, preferred_element_type=jnp.float32
    ) / math.sqrt(head_dim)
    live_mask = jnp.arange(key_rows.shape[0]) < cache_len[0]
    scores = jnp.where(live_mask, scores, -jnp.inf)
    row_top = jnp.max(scores, axis=-1, keepdims=True)
    lifted = jnp.exp(scores - row_top)
    row_total = jnp.sum(lifted, axis=-1)
    soft_weights = lifted.astype(jnp.bfloat16)
    mixed_heads = (
        jnp.einsum("rht,td->rhd", soft_weights, values, preferred_element_type=jnp.float32)
        / row_total[..., None]
    )
    attended = mixed_heads.reshape(group_rows, head_cols).astype(jnp.bfloat16)
    partial_value = jnp.dot(
        attended,
        lax.all_gather(out_weight, "attn", axis=1, tiled=True),
        preferred_element_type=jnp.float32,
    )
    summed = lax.psum_scatter(partial_value, ("sect", "pair"), scatter_dimension=0, tiled=True)
    mixed_f32 = residual.astype(jnp.float32) + summed
    mixed_rows = mixed_f32.astype(jnp.bfloat16)
    mixed_f32 = mixed_rows.astype(jnp.float32)
    normed = (
        mixed_f32
        * lax.rsqrt(jnp.mean(mixed_f32 * mixed_f32, axis=-1, keepdims=True) + 1e-06)
        * norm_gain
    ).astype(jnp.bfloat16)
    logits = jnp.dot(normed, router, preferred_element_type=jnp.float32)
    chosen_logits = jnp.take_along_axis(logits, expert_ids, axis=1)
    route_weights = jax.nn.softmax(chosen_logits, axis=-1)
    row_count, top_count = expert_ids.shape
    expert_count = router.shape[1]
    model_width = residual.shape[1]
    capacity = max(2, row_count * top_count // expert_count * 2)
    flat_ids = expert_ids.reshape(-1)
    onehot = (flat_ids[:, None] == jnp.arange(expert_count, dtype=jnp.int32)[None, :]).astype(
        jnp.int32
    )
    earlier = jnp.cumsum(onehot, axis=0) - onehot
    slot_index = jnp.sum(earlier * onehot, axis=1)
    source = jnp.repeat(jnp.arange(row_count, dtype=jnp.int32), top_count)
    outgoing = (
        jnp.zeros((expert_count, capacity, model_width), jnp.bfloat16)
        .at[flat_ids, slot_index]
        .set(normed[source])
    )
    received = lax.all_to_all(outgoing, ("attn", "pair"), split_axis=0, concat_axis=0, tiled=True)
    sections = lax.axis_size("sect")
    every_section = lax.all_gather(received, "sect", axis=0, tiled=True)
    tokens_in = every_section.reshape(-1, model_width)
    gate_val = jnp.dot(tokens_in, w_gate[0], preferred_element_type=jnp.float32)
    up_val = jnp.dot(tokens_in, w_up[0], preferred_element_type=jnp.float32)
    part_hidden = (jax.nn.silu(gate_val) * up_val).astype(jnp.bfloat16)
    hidden = lax.all_gather(part_hidden, "sect", axis=1, tiled=True)
    out_slice = jnp.dot(hidden, w_down[0], preferred_element_type=jnp.float32).astype(jnp.bfloat16)
    out_slice = out_slice.reshape(sections, expert_count, capacity, model_width // sections)
    segmented = lax.all_to_all(out_slice, "sect", split_axis=0, concat_axis=3, tiled=True)
    returned = lax.all_to_all(
        segmented[0], ("attn", "pair"), split_axis=0, concat_axis=0, tiled=True
    )
    gathered = (
        returned[flat_ids, slot_index]
        .reshape(row_count, top_count, model_width)
        .astype(jnp.float32)
    )
    joined = jnp.sum(route_weights[:, :, None] * gathered, axis=1)
    return (mixed_f32 + joined).astype(jnp.bfloat16)


def rotate(value, axis, step):
    size = lax.axis_size(axis)
    return lax.ppermute(value, axis, [(i, (i + step) % size) for i in range(size)])


def swap(value, axis, mask):
    size = lax.axis_size(axis)
    return lax.ppermute(value, axis, [(i, i ^ mask) for i in range(size)])


def anchor_kernel(out_ref):
    out_ref[...] = jnp.zeros_like(out_ref)


def pack_kernel(attn, sect, *refs):
    _, q_ref, kv_ref, list_ref, len_ref, res_ref, ids_ref, down_ref, *refs = refs
    own_ref, far_ref, near_ref, q_out, *downs = refs
    my_attn, my_sect = lax.axis_index("attn"), lax.axis_index("sect")
    q_out[...] = q_ref[...]
    ff = downs[0].shape[0]
    for i in range(sect):
        start = pl.multiple_of(lax.rem(my_sect + i, sect) * ff, ff)
        downs[i][...] = down_ref[pl.ds(start, ff), :]
    per_dev = res_ref.shape[0]
    top = ids_ref.shape[0]
    width = res_ref.shape[1] // attn
    _, blocks, keys, kv_cols = kv_ref.shape
    folds = width // kv_cols
    local_heads = HEADS // (lax.axis_size("sect") * lax.axis_size("pair"))
    kv_local = lax.axis_index("pair") * local_heads // (HEADS // KV_HEADS)
    lane = lax.broadcasted_iota(jnp.int32, (per_dev, kv_cols - 128), 1)
    facts = jnp.zeros((per_dev, kv_cols - 128), jnp.int32)
    list_len = list_ref.shape[1]
    for j in range(list_len):
        facts = jnp.where(lane == j, list_ref[:, j : j + 1], facts)
    facts = jnp.where(lane == list_len, len_ref[...] // 128, facts)
    facts = jnp.where(lane == list_len + 1, lax.rem(len_ref[...], 128), facts)
    facts = facts.astype(jnp.float32).astype(jnp.bfloat16)
    eye = (
        lax.broadcasted_iota(jnp.int32, (per_dev, per_dev), 0)
        == lax.broadcasted_iota(jnp.int32, (per_dev, per_dev), 1)
    )
    ids = lax.dot_general(
        eye.astype(jnp.float32).astype(jnp.bfloat16),
        ids_ref[...].astype(jnp.float32).astype(jnp.bfloat16),
        (((1,), (1,)), ((), ())),
        preferred_element_type=jnp.float32,
    )
    ids = jnp.concatenate([ids, jnp.zeros((per_dev, 128 - top), jnp.float32)], axis=1)
    named = jnp.concatenate([ids.astype(jnp.bfloat16), facts], axis=1)

    def put_slice(ref, row, receiver):
        for f in range(folds):
            start = pl.multiple_of(receiver * width + f * kv_cols, kv_cols)
            ref[row + f * per_dev : row + (f + 1) * per_dev, :] = res_ref[:, pl.ds(start, kv_cols)]

    first = folds * per_dev
    after = first + blocks * keys
    for ref, mask in ((own_ref, 0), (far_ref, 2), (near_ref, 1)):
        put_slice(ref, 0, my_attn ^ mask)
        for b in range(blocks):
            ref[first + b * keys : first + (b + 1) * keys, :] = kv_ref[kv_local, b]
        ref[after : after + per_dev, :] = named
    put_slice(far_ref, after + per_dev, my_attn ^ 3)


def attend_kernel(attn, sect, pair, list_len, blocks, keys, *refs):
    q_refs, refs = refs[:attn], refs[attn:]
    pack_refs, refs = refs[:attn], refs[attn:]
    w_ref, refs = refs[0], refs[1:]
    part_refs, refs = refs[:pair], refs[pair:]
    ids_ref, pool, attended, split = refs
    per_dev = ids_ref.shape[0]
    rows, head_cols = q_refs[0].shape
    kv_cols = pack_refs[0].shape[1]
    width = w_ref.shape[1]
    heads = head_cols // HEAD_DIM
    folds = width // kv_cols
    me, my_sect, my_pair = (lax.axis_index(n) for n in ("attn", "sect", "pair"))
    lane = lax.broadcasted_iota(jnp.int32, (1, kv_cols - 128), 1)
    cache_at = [0 if k == 3 else folds * per_dev for k in range(attn)]
    named_at = [at + blocks * keys for at in cache_at]
    slice_at = [named_at[k] + per_dev if k == 3 else 0 for k in range(attn)]
    lists, lives = [], []
    for k in range(attn):
        group = me ^ k
        for b in range(blocks):
            at = cache_at[k] + b * keys
            pool[group * blocks + b] = pack_refs[k][at : at + keys, :]
        facts = pack_refs[k][named_at[k] : named_at[k] + per_dev, 128:]
        facts = facts.astype(jnp.float32)[0:1, :]

        def fact(j, facts=facts):
            return jnp.sum(jnp.where(lane == j, facts, 0.0)).astype(jnp.int32)

        lists.append([fact(j) for j in range(list_len)])
        lives.append(fact(list_len) * 128 + fact(list_len + 1))
    for k in range(attn):
        group = me ^ k
        picked = [pool[index] for index in lists[k]]
        key_rows = jnp.concatenate([p[:, :HEAD_DIM] for p in picked], axis=0)
        values = jnp.concatenate([p[:, HEAD_DIM:] for p in picked], axis=0)
        q_all = q_refs[k][...]
        stacked = jnp.concatenate(
            [q_all[:, h * HEAD_DIM : (h + 1) * HEAD_DIM] for h in range(heads)], axis=0
        )
        scores = lax.dot_general(
            stacked, key_rows, (((1,), (1,)), ((), ())), preferred_element_type=jnp.float32
        ) / math.sqrt(HEAD_DIM)
        where = lax.broadcasted_iota(jnp.int32, scores.shape, 1)
        scores = jnp.where(where < lives[k], scores, -jnp.inf)
        top = jnp.max(scores, axis=-1, keepdims=True)
        lifted = jnp.exp(scores - top)
        total = jnp.sum(lifted, axis=-1, keepdims=True)
        mixed = (
            jnp.dot(lifted.astype(jnp.bfloat16), values, preferred_element_type=jnp.float32)
            / total
        ).astype(jnp.bfloat16)
        start = pl.multiple_of(group * rows, rows)
        for h in range(heads):
            attended[pl.ds(start, rows), h * HEAD_DIM : (h + 1) * HEAD_DIM] = mixed[
                h * rows : (h + 1) * rows, :
            ]
    product = jnp.dot(attended[...], w_ref[...], preferred_element_type=jnp.float32)
    for g in range(attn):
        for s in range(sect):
            for p in range(pair):
                source = g * rows + (s * pair + p) * per_dev
                target = (s * attn + g) * per_dev
                split[p, target : target + per_dev, :] = product[source : source + per_dev, :]
    for k in range(attn):
        group = me ^ k
        target = pl.ds(pl.multiple_of((my_sect * attn + group) * per_dev, per_dev), per_dev)
        for f in range(folds):
            at = slice_at[k] + f * per_dev
            split[my_pair, target, f * kv_cols : (f + 1) * kv_cols] += pack_refs[k][
                at : at + per_dev, :
            ].astype(jnp.float32)
        lanes = pl.ds(pl.multiple_of(group * 128, 128), 128)
        ids_ref[:, lanes] = pack_refs[k][named_at[k] : named_at[k] + per_dev, :128]
    for i in range(pair):
        part_refs[i][...] = split[lax.rem(my_pair + i, pair)]


def pair_sum_kernel(sect, pair, kept_ref, *refs):
    came, ids_ref, refs = refs[: pair - 1], refs[pair - 1], refs[pair:]
    totals, sents = refs[:sect], refs[sect:]
    my_sect = lax.axis_index("sect")
    part = kept_ref.shape[0] // sect
    for i in range(sect):
        rows = pl.ds(pl.multiple_of(lax.rem(my_sect + i, sect) * part, part), part)
        total = kept_ref[rows, :]
        for ref in came:
            total = total + ref[rows, :]
        totals[i][...] = total
        sents[i][:part, :] = total.astype(jnp.bfloat16)
    named = ids_ref.shape[1]
    sents[0][part:, :named] = ids_ref[...]
    if named < kept_ref.shape[1]:
        sents[0][part:, named:] = jnp.zeros(
            (ids_ref.shape[0], kept_ref.shape[1] - named), jnp.bfloat16
        )


def sect_sum_kernel(kept_ref, names_ref, *refs):
    *came, mixed_ref, sent_ref = refs
    part = kept_ref.shape[0]
    total = kept_ref[...]
    for ref in came:
        total = total + ref[:part, :].astype(jnp.float32)
    mixed = total.astype(jnp.bfloat16)
    mixed_ref[...] = mixed
    sent_ref[:part, :] = mixed
    sent_ref[part:, :] = names_ref[part:, :]


def expert_kernel(attn, sect, pair, per_dev, top, *refs):
    piece_refs, refs = refs[: attn * pair], refs[attn * pair :]
    gain_ref, router_ref, gate_ref, up_ref, refs = *refs[:4], refs[4:]
    down_refs, refs = refs[:sect], refs[sect:]
    part_refs, refs = refs[:pair], refs[pair:]
    own_refs, (ids_all, contribution) = refs[:-2], refs[-2:]
    part = attn * per_dev
    width = piece_refs[0].shape[1]
    model = width * attn
    me, my_sect, my_pair = (lax.axis_index(n) for n in ("attn", "sect", "pair"))
    my_expert = me * pair + my_pair
    rows = part * pair
    values = []
    squares = jnp.zeros((rows, 1), jnp.float32)
    for k in range(attn):
        value = jnp.concatenate(
            [piece_refs[j * attn + k][:part, :] for j in range(pair)], axis=0
        ).astype(jnp.float32)
        values.append(value)
        squares = squares + jnp.sum(value * value, axis=-1, keepdims=True)
    scale = lax.rsqrt(squares / model + 1e-06)
    gate = up = logits = None
    own_start = pl.multiple_of(me * per_dev, per_dev)
    for k in range(attn):
        group = me ^ k
        cols = pl.ds(pl.multiple_of(group * width, width), width)
        lines = width // 128
        gain = jnp.concatenate(
            [gain_ref[pl.ds(group * lines + j, 1), :] for j in range(lines)], axis=1
        )
        normed = (values[k] * scale * gain).astype(jnp.bfloat16)
        parts = [
            jnp.dot(normed, ref[cols, :], preferred_element_type=jnp.float32)
            for ref in (gate_ref, up_ref)
        ] + [
            lax.dot_general(
                normed,
                router_ref[:, cols],
                (((1,), (1,)), ((), ())),
                preferred_element_type=jnp.float32,
            )
        ]
        if k == 0:
            gate, up, logits = parts
        else:
            gate, up, logits = gate + parts[0], up + parts[1], logits + parts[2]
        for own_ref in own_refs:
            own_ref[:, cols] = piece_refs[k][pl.ds(own_start, per_dev), :]
    for j in range(pair):
        block = piece_refs[j * attn][part:, :].astype(jnp.float32)
        for g in range(attn):
            target = j * part + g * per_dev
            ids_all[target : target + per_dev, :] = block[:, g * 128 : g * 128 + top]
    ids = ids_all[...]
    lane = lax.broadcasted_iota(jnp.int32, logits.shape, 1)
    lane_f = lane.astype(jnp.float32)
    named = lane < 0
    for c in range(top):
        named = named | (ids[:, c : c + 1] == lane_f)
    chosen = jnp.where(named, logits, -jnp.inf)
    lifted = jnp.exp(chosen - jnp.max(chosen, axis=-1, keepdims=True))
    weights = lifted / jnp.sum(lifted, axis=-1, keepdims=True)
    weight = jnp.sum(jnp.where(lane == my_expert, weights, 0.0), axis=-1, keepdims=True)
    hidden = (gate / (1.0 + jnp.exp(-gate)) * up).astype(jnp.bfloat16)
    columns = down_refs[0].shape[1]
    for i in range(sect):
        from_sect = lax.rem(my_sect + sect - i, sect)
        cols = pl.ds(pl.multiple_of(from_sect * columns, columns), columns)
        contribution[:, cols] = (
            jnp.dot(hidden, down_refs[i][...], preferred_element_type=jnp.float32) * weight
        )
    part_refs[0][...] = contribution[:part, :]
    for j in range(1, pair):
        part_refs[j][...] = contribution[j * part : (j + 1) * part, :].astype(jnp.bfloat16)


def sum_kernel(kept_ref, *refs):
    *came, out_ref = refs
    total = kept_ref[...]
    for ref in came:
        total = total + ref[...].astype(jnp.float32)
    out_ref[...] = total.astype(out_ref.dtype)


def split_kernel(attn, kept_ref, *refs):
    came, outs = refs[:-attn], refs[-attn:]
    me = lax.axis_index("attn")
    part = kept_ref.shape[0] // attn
    for i in range(attn):
        rows = pl.ds(pl.multiple_of((me ^ i) * part, part), part)
        total = kept_ref[rows, :]
        for ref in came:
            total = total + ref[rows, :].astype(jnp.float32)
        outs[i][...] = total.astype(outs[i].dtype)


def call(kernel, operands, outs, scratch=(), limit=4 << 20, flops=1 << 20):
    moved = sum(x.size * x.dtype.itemsize for x in operands)
    return pl.pallas_call(
        kernel,
        out_shape=outs,
        in_specs=[VMEM] * len(operands),
        out_specs=jax.tree.map(lambda _: VMEM, outs),
        scratch_shapes=list(scratch),
        compiler_params=pltpu.CompilerParams(vmem_limit_bytes=limit),
        cost_estimate=pl.CostEstimate(flops=flops, bytes_accessed=moved, transcendentals=0),
    )(*operands)


def dense_layer(
    queries,
    kv_pool,
    block_list,
    cache_len,
    out_weight,
    residual,
    norm_gain,
    router,
    expert_ids,
    w_gate,
    w_up,
    w_down,
):
    attn, sect, pair = (lax.axis_size(n) for n in ("attn", "sect", "pair"))
    bf16, f32 = jnp.bfloat16, jnp.float32
    shape = jax.ShapeDtypeStruct
    rows, head_cols = queries.shape
    per_dev, model = residual.shape
    top = expert_ids.shape[1]
    width = out_weight.shape[1]
    ff = w_gate.shape[2]
    list_len = block_list.shape[1]
    _, blocks, keys, kv_cols = kv_pool.shape
    half = attn * sect * per_dev
    slice_rows = per_dev * width // kv_cols
    packed = slice_rows + blocks * keys + per_dev

    anchor = call(anchor_kernel, [], shape((8, 128), f32), flops=1 << 34)
    own_pack, far_pack, near_pack, own_q, *downs = call(
        functools.partial(pack_kernel, attn, sect),
        [
            anchor,
            queries,
            kv_pool,
            block_list,
            cache_len.reshape(1, 1),
            residual,
            expert_ids.T,
            w_down[0],
        ],
        [
            shape((packed, kv_cols), bf16),
            shape((packed + slice_rows, kv_cols), bf16),
            shape((packed, kv_cols), bf16),
            shape(queries.shape, bf16),
        ]
        + [shape((ff, w_down.shape[2]), bf16)] * sect,
    )
    far_pack = swap(far_pack, "attn", 2)
    far_q = swap(own_q, "attn", 2)
    downs = [downs[0]] + [rotate(downs[i], "sect", i) for i in range(1, sect)]
    near_pack = swap(near_pack, "attn", 1)
    near_q = swap(own_q, "attn", 1)
    last_pack = swap(far_pack[slice_rows:], "attn", 1)
    last_q = swap(far_q, "attn", 1)
    q = [own_q, near_q, far_q, last_q]
    packs = [own_pack, near_pack, far_pack, last_pack]

    parts = call(
        functools.partial(
            attend_kernel, attn, sect, pair, list_len, blocks, keys
        ),
        q + packs + [out_weight],
        [shape((half, width), f32)] * pair + [shape((per_dev, attn * 128), bf16)],
        [
            pltpu.VMEM((attn * blocks, keys, kv_cols), bf16),
            pltpu.VMEM((attn * rows, head_cols), bf16),
            pltpu.VMEM((pair, half, width), f32),
        ],
        limit=16 << 20,
    )
    part = attn * per_dev
    sums = call(
        functools.partial(pair_sum_kernel, sect, pair),
        [parts[0]]
        + [rotate(parts[j], "pair", j) for j in range(1, pair)]
        + [parts[pair]],
        [shape((part, width), f32)] * sect
        + [shape((part + per_dev, width), bf16)]
        + [shape((part, width), bf16)] * (sect - 1),
    )
    totals, sents = sums[:sect], sums[sect:]
    theirs = [rotate(sents[0], "sect", sect - i) for i in range(1, sect)]
    mine = [rotate(sents[i], "sect", i) for i in range(1, sect)]
    operands = [norm_gain.reshape(-1, 128), router.T, w_gate[0], w_up[0]] + downs

    def experts(shift):
        if shift == 0:
            names, came = sents[0], mine
        else:
            names, came = theirs[shift - 1], [theirs[shift - 1]]
        mixed, named = call(
            sect_sum_kernel,
            [totals[shift], names] + came,
            [shape((part, width), bf16), shape((part + per_dev, width), bf16)],
        )
        piece = {0: named}
        for k in range(1, attn):
            piece[k] = swap(mixed, "attn", k)
        pieces = [piece[k] for k in range(attn)]
        for j in range(1, pair):
            pieces += [rotate(piece[k], "pair", j) for k in range(attn)]
        outs = call(
            functools.partial(expert_kernel, attn, sect, pair, per_dev, top),
            pieces + operands,
            [shape((part, model), f32)]
            + [shape((part, model), bf16)] * (pair - 1)
            + [shape((per_dev, model), bf16)] * (shift == 0),
            [pltpu.VMEM((part * pair, top), f32), pltpu.VMEM((part * pair, model), f32)],
            limit=16 << 20,
            flops=1 << 31,
        )
        came = [rotate(outs[j], "pair", pair - j) for j in range(1, pair)]
        return outs, came

    def reduced(shift):
        outs, came = experts(shift)
        sums = call(
            functools.partial(split_kernel, attn),
            [outs[0]] + came,
            [shape((per_dev, model), f32)] + [shape((per_dev, model), bf16)] * (attn - 1),
        )
        home = [swap(sums[k], "attn", k) for k in range(1, attn)]
        return outs, sums[0], home

    from_sect = []
    for i in range(1, sect):
        _, own, home = reduced(i)
        sent = call(sum_kernel, [own] + home, shape((per_dev, model), bf16))
        from_sect.append(rotate(sent, "sect", i))
    outs, own, home = reduced(0)
    total = outs[pair].astype(f32) + own
    for came in home + from_sect:
        total = total + came.astype(f32)
    return total.astype(bf16)


def on_device(*operands):
    queries, expert_ids, router = operands[0], operands[8], operands[7]
    row_count, top_count = expert_ids.shape
    capacity = max(2, row_count * top_count // router.shape[1] * 2)
    local_heads = queries.shape[1] // HEAD_DIM
    one_each = operands[9].shape[0] == 1 and lax.axis_size("attn") == 4
    if capacity >= row_count and one_each and local_heads <= HEADS // KV_HEADS:
        return dense_layer(*operands)
    return routed_layer(*operands)


def solution(mesh):
    placed = (
        P(("group", "attn"), ("sect", "pair")),
        P("sect", ("group", "attn"), None, None),
        P(("group", "attn"), None),
        P(("group", "attn")),
        P(("sect", "pair"), "attn"),
        P(("group", "attn", "sect", "pair"), None),
        P(),
        P(),
        P(("group", "attn", "sect", "pair"), None),
        P(("attn", "pair"), None, "sect"),
        P(("attn", "pair"), None, "sect"),
        P(("attn", "pair"), None, "sect"),
    )
    return jax.shard_map(
        on_device,
        mesh=mesh,
        in_specs=placed,
        out_specs=P(("group", "attn", "sect", "pair"), None),
        check_vma=False,
    )
```

```python
import functools
import math

import jax
import jax.numpy as jnp
from jax import lax
from jax.experimental import pallas as pl
from jax.experimental.pallas import tpu as pltpu
from jax.sharding import PartitionSpec as P


HEADS = 32
KV_HEADS = 4
HEAD_DIM = 128


VMEM = pl.BlockSpec(memory_space=pltpu.VMEM)


def routed_layer(
    queries,
    kv_pool,
    block_list,
    cache_len,
    out_weight,
    residual,
    norm_gain,
    router,
    expert_ids,
    w_gate,
    w_up,
    w_down,
):
    head_dim = HEAD_DIM
    per_kv = HEADS // KV_HEADS
    group_rows, head_cols = queries.shape
    local_heads = head_cols // head_dim
    pool_all = lax.all_gather(kv_pool, "attn", axis=1, tiled=True)
    picked = jnp.take(pool_all, block_list[0], axis=1)
    kv_local = lax.axis_index("pair") * local_heads // per_kv
    chosen = lax.dynamic_index_in_dim(picked, kv_local, 0, keepdims=False)
    chosen = chosen.reshape(-1, 2 * head_dim)
    key_rows = chosen[:, :head_dim]
    values = chosen[:, head_dim:]
    query_heads = queries.reshape(group_rows, local_heads, head_dim)
    scores = jnp.einsum(
        "rhd,td->rht", query_heads, key_rows, preferred_element_type=jnp.float32
    ) / math.sqrt(head_dim)
    live_mask = jnp.arange(key_rows.shape[0]) < cache_len[0]
    scores = jnp.where(live_mask, scores, -jnp.inf)
    row_top = jnp.max(scores, axis=-1, keepdims=True)
    lifted = jnp.exp(scores - row_top)
    row_total = jnp.sum(lifted, axis=-1)
    soft_weights = lifted.astype(jnp.bfloat16)
    mixed_heads = (
        jnp.einsum("rht,td->rhd", soft_weights, values, preferred_element_type=jnp.float32)
        / row_total[..., None]
    )
    attended = mixed_heads.reshape(group_rows, head_cols).astype(jnp.bfloat16)
    partial_value = jnp.dot(
        attended,
        lax.all_gather(out_weight, "attn", axis=1, tiled=True),
        preferred_element_type=jnp.float32,
    )
    summed = lax.psum_scatter(partial_value, ("sect", "pair"), scatter_dimension=0, tiled=True)
    mixed_f32 = residual.astype(jnp.float32) + summed
    mixed_rows = mixed_f32.astype(jnp.bfloat16)
    mixed_f32 = mixed_rows.astype(jnp.float32)
    normed = (
        mixed_f32
        * lax.rsqrt(jnp.mean(mixed_f32 * mixed_f32, axis=-1, keepdims=True) + 1e-06)
        * norm_gain
    ).astype(jnp.bfloat16)
    logits = jnp.dot(normed, router, preferred_element_type=jnp.float32)
    chosen_logits = jnp.take_along_axis(logits, expert_ids, axis=1)
    route_weights = jax.nn.softmax(chosen_logits, axis=-1)
    row_count, top_count = expert_ids.shape
    expert_count = router.shape[1]
    model_width = residual.shape[1]
    capacity = max(2, row_count * top_count // expert_count * 2)
    flat_ids = expert_ids.reshape(-1)
    onehot = (flat_ids[:, None] == jnp.arange(expert_count, dtype=jnp.int32)[None, :]).astype(
        jnp.int32
    )
    earlier = jnp.cumsum(onehot, axis=0) - onehot
    slot_index = jnp.sum(earlier * onehot, axis=1)
    source = jnp.repeat(jnp.arange(row_count, dtype=jnp.int32), top_count)
    outgoing = (
        jnp.zeros((expert_count, capacity, model_width), jnp.bfloat16)
        .at[flat_ids, slot_index]
        .set(normed[source])
    )
    received = lax.all_to_all(outgoing, ("attn", "pair"), split_axis=0, concat_axis=0, tiled=True)
    sections = lax.axis_size("sect")
    every_section = lax.all_gather(received, "sect", axis=0, tiled=True)
    tokens_in = every_section.reshape(-1, model_width)
    gate_val = jnp.dot(tokens_in, w_gate[0], preferred_element_type=jnp.float32)
    up_val = jnp.dot(tokens_in, w_up[0], preferred_element_type=jnp.float32)
    part_hidden = (jax.nn.silu(gate_val) * up_val).astype(jnp.bfloat16)
    hidden = lax.all_gather(part_hidden, "sect", axis=1, tiled=True)
    out_slice = jnp.dot(hidden, w_down[0], preferred_element_type=jnp.float32).astype(jnp.bfloat16)
    out_slice = out_slice.reshape(sections, expert_count, capacity, model_width // sections)
    segmented = lax.all_to_all(out_slice, "sect", split_axis=0, concat_axis=3, tiled=True)
    returned = lax.all_to_all(
        segmented[0], ("attn", "pair"), split_axis=0, concat_axis=0, tiled=True
    )
    gathered = (
        returned[flat_ids, slot_index]
        .reshape(row_count, top_count, model_width)
        .astype(jnp.float32)
    )
    joined = jnp.sum(route_weights[:, :, None] * gathered, axis=1)
    return (mixed_f32 + joined).astype(jnp.bfloat16)


def rotate(value, axis, step):
    size = lax.axis_size(axis)
    return lax.ppermute(value, axis, [(i, (i + step) % size) for i in range(size)])


def swap(value, axis, mask):
    size = lax.axis_size(axis)
    return lax.ppermute(value, axis, [(i, i ^ mask) for i in range(size)])


def anchor_kernel(out_ref):
    out_ref[...] = jnp.zeros_like(out_ref)


def pack_kernel(attn, sect, *refs):
    _, kv_ref, list_ref, len_ref, res_ref, ids_ref, down_ref, *refs = refs
    own_ref, far_ref, near_ref, *downs = refs
    my_attn, my_sect = lax.axis_index("attn"), lax.axis_index("sect")
    ff = downs[0].shape[0]
    for i in range(sect):
        start = pl.multiple_of(lax.rem(my_sect + i, sect) * ff, ff)
        downs[i][...] = down_ref[pl.ds(start, ff), :]
    per_dev = res_ref.shape[0]
    top = ids_ref.shape[0]
    width = res_ref.shape[1] // attn
    _, blocks, keys, kv_cols = kv_ref.shape
    folds = width // kv_cols
    local_heads = HEADS // (lax.axis_size("sect") * lax.axis_size("pair"))
    kv_local = lax.axis_index("pair") * local_heads // (HEADS // KV_HEADS)
    lane = lax.broadcasted_iota(jnp.int32, (per_dev, kv_cols - 128), 1)
    facts = jnp.zeros((per_dev, kv_cols - 128), jnp.int32)
    list_len = list_ref.shape[1]
    for j in range(list_len):
        facts = jnp.where(lane == j, list_ref[:, j : j + 1], facts)
    length = jnp.broadcast_to(len_ref[...], (per_dev, 1))
    facts = jnp.where(lane == list_len, length // 128, facts)
    facts = jnp.where(lane == list_len + 1, lax.rem(length, 128), facts)
    facts = facts.astype(jnp.float32).astype(jnp.bfloat16)
    eye = (
        lax.broadcasted_iota(jnp.int32, (per_dev, per_dev), 0)
        == lax.broadcasted_iota(jnp.int32, (per_dev, per_dev), 1)
    )
    ids = lax.dot_general(
        eye.astype(jnp.float32).astype(jnp.bfloat16),
        ids_ref[...].astype(jnp.float32).astype(jnp.bfloat16),
        (((1,), (1,)), ((), ())),
        preferred_element_type=jnp.float32,
    )
    ids = jnp.concatenate([ids, jnp.zeros((per_dev, 128 - top), jnp.float32)], axis=1)
    named = jnp.concatenate([ids.astype(jnp.bfloat16), facts], axis=1)

    def put_slice(ref, row, receiver):
        for f in range(folds):
            start = pl.multiple_of(receiver * width + f * kv_cols, kv_cols)
            ref[row + f * per_dev : row + (f + 1) * per_dev, :] = res_ref[:, pl.ds(start, kv_cols)]

    first = folds * per_dev
    after = first + blocks * keys
    for ref, mask in ((own_ref, 0), (far_ref, 2), (near_ref, 1)):
        put_slice(ref, 0, my_attn ^ mask)
        for b in range(blocks):
            ref[first + b * keys : first + (b + 1) * keys, :] = kv_ref[kv_local, b]
        ref[after : after + per_dev, :] = named
    put_slice(far_ref, after + per_dev, my_attn ^ 3)


def attend_kernel(attn, sect, pair, list_len, blocks, keys, *refs):
    q_refs, refs = refs[:attn], refs[attn:]
    pack_refs, refs = refs[:attn], refs[attn:]
    w_ref, refs = refs[0], refs[1:]
    part_refs, refs = refs[:pair], refs[pair:]
    ids_ref, pool, attended, split = refs
    per_dev = ids_ref.shape[0]
    rows, head_cols = q_refs[0].shape
    kv_cols = pack_refs[0].shape[1]
    width = w_ref.shape[1]
    heads = head_cols // HEAD_DIM
    folds = width // kv_cols
    me, my_sect, my_pair = (lax.axis_index(n) for n in ("attn", "sect", "pair"))
    lane = lax.broadcasted_iota(jnp.int32, (1, kv_cols - 128), 1)
    cache_at = [0 if k == 3 else folds * per_dev for k in range(attn)]
    named_at = [at + blocks * keys for at in cache_at]
    slice_at = [named_at[k] + per_dev if k == 3 else 0 for k in range(attn)]
    lists, lives = [], []
    for k in range(attn):
        group = me ^ k
        for b in range(blocks):
            at = cache_at[k] + b * keys
            pool[group * blocks + b] = pack_refs[k][at : at + keys, :]
        facts = pack_refs[k][named_at[k] : named_at[k] + per_dev, 128:]
        facts = facts.astype(jnp.float32)[0:1, :]

        def fact(j, facts=facts):
            return jnp.sum(jnp.where(lane == j, facts, 0.0)).astype(jnp.int32)

        lists.append([fact(j) for j in range(list_len)])
        lives.append(fact(list_len) * 128 + fact(list_len + 1))
    for k in range(attn):
        group = me ^ k
        picked = [pool[index] for index in lists[k]]
        key_rows = jnp.concatenate([p[:, :HEAD_DIM] for p in picked], axis=0)
        values = jnp.concatenate([p[:, HEAD_DIM:] for p in picked], axis=0)
        q_all = q_refs[k][...]
        stacked = jnp.concatenate(
            [q_all[:, h * HEAD_DIM : (h + 1) * HEAD_DIM] for h in range(heads)], axis=0
        )
        scores = lax.dot_general(
            stacked, key_rows, (((1,), (1,)), ((), ())), preferred_element_type=jnp.float32
        ) / math.sqrt(HEAD_DIM)
        where = lax.broadcasted_iota(jnp.int32, scores.shape, 1)
        scores = jnp.where(where < lives[k], scores, -jnp.inf)
        top = jnp.max(scores, axis=-1, keepdims=True)
        lifted = jnp.exp(scores - top)
        total = jnp.sum(lifted, axis=-1, keepdims=True)
        mixed = (
            jnp.dot(lifted.astype(jnp.bfloat16), values, preferred_element_type=jnp.float32)
            / total
        ).astype(jnp.bfloat16)
        start = pl.multiple_of(group * rows, rows)
        for h in range(heads):
            attended[pl.ds(start, rows), h * HEAD_DIM : (h + 1) * HEAD_DIM] = mixed[
                h * rows : (h + 1) * rows, :
            ]
    product = jnp.dot(attended[...], w_ref[...], preferred_element_type=jnp.float32)
    for g in range(attn):
        for s in range(sect):
            for p in range(pair):
                source = g * rows + (s * pair + p) * per_dev
                target = (s * attn + g) * per_dev
                split[p, target : target + per_dev, :] = product[source : source + per_dev, :]
    for k in range(attn):
        group = me ^ k
        target = pl.ds(pl.multiple_of((my_sect * attn + group) * per_dev, per_dev), per_dev)
        for f in range(folds):
            at = slice_at[k] + f * per_dev
            split[my_pair, target, f * kv_cols : (f + 1) * kv_cols] += pack_refs[k][
                at : at + per_dev, :
            ].astype(jnp.float32)
        lanes = pl.ds(pl.multiple_of(group * 128, 128), 128)
        ids_ref[:, lanes] = pack_refs[k][named_at[k] : named_at[k] + per_dev, :128]
    for i in range(pair):
        part_refs[i][...] = split[lax.rem(my_pair + i, pair)]


def pair_sum_kernel(sect, pair, kept_ref, *refs):
    came, ids_ref, refs = refs[: pair - 1], refs[pair - 1], refs[pair:]
    totals, sents = refs[:sect], refs[sect:]
    my_sect = lax.axis_index("sect")
    part = kept_ref.shape[0] // sect
    for i in range(sect):
        rows = pl.ds(pl.multiple_of(lax.rem(my_sect + i, sect) * part, part), part)
        total = kept_ref[rows, :]
        for ref in came:
            total = total + ref[rows, :]
        totals[i][...] = total
        sents[i][:part, :] = total.astype(jnp.bfloat16)
    named = ids_ref.shape[1]
    sents[0][part:, :named] = ids_ref[...]
    if named < kept_ref.shape[1]:
        sents[0][part:, named:] = jnp.zeros(
            (ids_ref.shape[0], kept_ref.shape[1] - named), jnp.bfloat16
        )


def sect_sum_kernel(kept_ref, names_ref, *refs):
    *came, mixed_ref, sent_ref = refs
    part = kept_ref.shape[0]
    total = kept_ref[...]
    for ref in came:
        total = total + ref[:part, :].astype(jnp.float32)
    mixed = total.astype(jnp.bfloat16)
    mixed_ref[...] = mixed
    sent_ref[:part, :] = mixed
    sent_ref[part:, :] = names_ref[part:, :]


def expert_kernel(attn, sect, pair, per_dev, top, *refs):
    piece_refs, refs = refs[: attn * pair], refs[attn * pair :]
    gain_ref, router_ref, gate_ref, up_ref, refs = *refs[:4], refs[4:]
    down_refs, refs = refs[:sect], refs[sect:]
    part_refs, refs = refs[:pair], refs[pair:]
    own_refs, (ids_all, contribution) = refs[:-2], refs[-2:]
    part = attn * per_dev
    width = piece_refs[0].shape[1]
    model = width * attn
    me, my_sect, my_pair = (lax.axis_index(n) for n in ("attn", "sect", "pair"))
    my_expert = me * pair + my_pair
    rows = part * pair
    values = []
    squares = jnp.zeros((rows, 1), jnp.float32)
    for k in range(attn):
        value = jnp.concatenate(
            [piece_refs[j * attn + k][:part, :] for j in range(pair)], axis=0
        ).astype(jnp.float32)
        values.append(value)
        squares = squares + jnp.sum(value * value, axis=-1, keepdims=True)
    scale = lax.rsqrt(squares / model + 1e-06)
    gate = up = logits = None
    own_start = pl.multiple_of(me * per_dev, per_dev)
    for k in range(attn):
        group = me ^ k
        cols = pl.ds(pl.multiple_of(group * width, width), width)
        lines = width // 128
        gain = jnp.concatenate(
            [gain_ref[pl.ds(group * lines + j, 1), :] for j in range(lines)], axis=1
        )
        normed = (values[k] * scale * gain).astype(jnp.bfloat16)
        parts = [
            jnp.dot(normed, ref[cols, :], preferred_element_type=jnp.float32)
            for ref in (gate_ref, up_ref)
        ] + [
            lax.dot_general(
                normed,
                router_ref[:, cols],
                (((1,), (1,)), ((), ())),
                preferred_element_type=jnp.float32,
            )
        ]
        if k == 0:
            gate, up, logits = parts
        else:
            gate, up, logits = gate + parts[0], up + parts[1], logits + parts[2]
        for own_ref in own_refs:
            own_ref[:, cols] = piece_refs[k][pl.ds(own_start, per_dev), :]
    for j in range(pair):
        block = piece_refs[j * attn][part:, :].astype(jnp.float32)
        for g in range(attn):
            target = j * part + g * per_dev
            ids_all[target : target + per_dev, :] = block[:, g * 128 : g * 128 + top]
    ids = ids_all[...]
    lane = lax.broadcasted_iota(jnp.int32, logits.shape, 1)
    lane_f = lane.astype(jnp.float32)
    named = lane < 0
    for c in range(top):
        named = named | (ids[:, c : c + 1] == lane_f)
    chosen = jnp.where(named, logits, -jnp.inf)
    lifted = jnp.exp(chosen - jnp.max(chosen, axis=-1, keepdims=True))
    weights = lifted / jnp.sum(lifted, axis=-1, keepdims=True)
    weight = jnp.sum(jnp.where(lane == my_expert, weights, 0.0), axis=-1, keepdims=True)
    hidden = (gate / (1.0 + jnp.exp(-gate)) * up).astype(jnp.bfloat16)
    columns = down_refs[0].shape[1]
    for i in range(sect):
        from_sect = lax.rem(my_sect + sect - i, sect)
        cols = pl.ds(pl.multiple_of(from_sect * columns, columns), columns)
        contribution[:, cols] = (
            jnp.dot(hidden, down_refs[i][...], preferred_element_type=jnp.float32) * weight
        )
    part_refs[0][...] = contribution[:part, :]
    for j in range(1, pair):
        part_refs[j][...] = contribution[j * part : (j + 1) * part, :].astype(jnp.bfloat16)


def sum_kernel(kept_ref, *refs):
    *came, out_ref = refs
    total = kept_ref[...]
    for ref in came:
        total = total + ref[...].astype(jnp.float32)
    out_ref[...] = total.astype(out_ref.dtype)


def split_kernel(attn, kept_ref, *refs):
    came, outs = refs[:-attn], refs[-attn:]
    me = lax.axis_index("attn")
    part = kept_ref.shape[0] // attn
    for i in range(attn):
        rows = pl.ds(pl.multiple_of((me ^ i) * part, part), part)
        total = kept_ref[rows, :]
        for ref in came:
            total = total + ref[rows, :].astype(jnp.float32)
        outs[i][...] = total.astype(outs[i].dtype)


def call(kernel, operands, outs, scratch=(), limit=4 << 20, flops=1 << 20):
    moved = sum(x.size * x.dtype.itemsize for x in operands)
    return pl.pallas_call(
        kernel,
        out_shape=outs,
        in_specs=[VMEM] * len(operands),
        out_specs=jax.tree.map(lambda _: VMEM, outs),
        scratch_shapes=list(scratch),
        compiler_params=pltpu.CompilerParams(vmem_limit_bytes=limit),
        cost_estimate=pl.CostEstimate(flops=flops, bytes_accessed=moved, transcendentals=0),
    )(*operands)


def dense_layer(
    queries,
    kv_pool,
    block_list,
    cache_len,
    out_weight,
    residual,
    norm_gain,
    router,
    expert_ids,
    w_gate,
    w_up,
    w_down,
):
    attn, sect, pair = (lax.axis_size(n) for n in ("attn", "sect", "pair"))
    bf16, f32 = jnp.bfloat16, jnp.float32
    shape = jax.ShapeDtypeStruct
    rows, head_cols = queries.shape
    per_dev, model = residual.shape
    top = expert_ids.shape[1]
    width = out_weight.shape[1]
    ff = w_gate.shape[2]
    list_len = block_list.shape[1]
    _, blocks, keys, kv_cols = kv_pool.shape
    half = attn * sect * per_dev
    slice_rows = per_dev * width // kv_cols
    packed = slice_rows + blocks * keys + per_dev

    anchor = call(anchor_kernel, [], shape((8, 128), f32), flops=1 << 34)
    far_q = swap(queries, "attn", 2)
    near_q = swap(queries, "attn", 1)
    own_pack, far_pack, near_pack, *downs = call(
        functools.partial(pack_kernel, attn, sect),
        [
            anchor,
            kv_pool,
            block_list,
            cache_len,
            residual,
            expert_ids.T,
            w_down[0],
        ],
        [
            shape((packed, kv_cols), bf16),
            shape((packed + slice_rows, kv_cols), bf16),
            shape((packed, kv_cols), bf16),
        ]
        + [shape((ff, w_down.shape[2]), bf16)] * sect,
    )
    far_pack = swap(far_pack, "attn", 2)
    downs = [downs[0]] + [rotate(downs[i], "sect", i) for i in range(1, sect)]
    near_pack = swap(near_pack, "attn", 1)
    last_pack = swap(far_pack[slice_rows:], "attn", 1)
    last_q = swap(far_q, "attn", 1)
    q = [queries, near_q, far_q, last_q]
    packs = [own_pack, near_pack, far_pack, last_pack]

    parts = call(
        functools.partial(
            attend_kernel, attn, sect, pair, list_len, blocks, keys
        ),
        q + packs + [out_weight],
        [shape((half, width), f32)] * pair + [shape((per_dev, attn * 128), bf16)],
        [
            pltpu.VMEM((attn * blocks, keys, kv_cols), bf16),
            pltpu.VMEM((attn * rows, head_cols), bf16),
            pltpu.VMEM((pair, half, width), f32),
        ],
        limit=16 << 20,
    )
    part = attn * per_dev
    sums = call(
        functools.partial(pair_sum_kernel, sect, pair),
        [parts[0]]
        + [rotate(parts[j], "pair", j) for j in range(1, pair)]
        + [parts[pair]],
        [shape((part, width), f32)] * sect
        + [shape((part + per_dev, width), bf16)]
        + [shape((part, width), bf16)] * (sect - 1),
    )
    totals, sents = sums[:sect], sums[sect:]
    theirs = [rotate(sents[0], "sect", sect - i) for i in range(1, sect)]
    mine = [rotate(sents[i], "sect", i) for i in range(1, sect)]
    operands = [norm_gain.reshape(-1, 128), router.T, w_gate[0], w_up[0]] + downs

    def experts(shift):
        if shift == 0:
            names, came = sents[0], mine
        else:
            names, came = theirs[shift - 1], [theirs[shift - 1]]
        mixed, named = call(
            sect_sum_kernel,
            [totals[shift], names] + came,
            [shape((part, width), bf16), shape((part + per_dev, width), bf16)],
        )
        piece = {0: named}
        for k in range(1, attn):
            piece[k] = swap(mixed, "attn", k)
        pieces = [piece[k] for k in range(attn)]
        for j in range(1, pair):
            pieces += [rotate(piece[k], "pair", j) for k in range(attn)]
        outs = call(
            functools.partial(expert_kernel, attn, sect, pair, per_dev, top),
            pieces + operands,
            [shape((part, model), f32)]
            + [shape((part, model), bf16)] * (pair - 1)
            + [shape((per_dev, model), bf16)] * (shift == 0),
            [pltpu.VMEM((part * pair, top), f32), pltpu.VMEM((part * pair, model), f32)],
            limit=16 << 20,
            flops=1 << 31,
        )
        came = [rotate(outs[j], "pair", pair - j) for j in range(1, pair)]
        return outs, came

    def reduced(shift):
        outs, came = experts(shift)
        sums = call(
            functools.partial(split_kernel, attn),
            [outs[0]] + came,
            [shape((per_dev, model), f32)] + [shape((per_dev, model), bf16)] * (attn - 1),
        )
        home = [swap(sums[k], "attn", k) for k in range(1, attn)]
        return outs, sums[0], home

    from_sect = []
    for i in range(1, sect):
        _, own, home = reduced(i)
        sent = call(sum_kernel, [own] + home, shape((per_dev, model), bf16))
        from_sect.append(rotate(sent, "sect", i))
    outs, own, home = reduced(0)
    total = outs[pair].astype(f32) + own
    for came in home + from_sect:
        total = total + came.astype(f32)
    return total.astype(bf16)


def on_device(*operands):
    queries, expert_ids, router = operands[0], operands[8], operands[7]
    row_count, top_count = expert_ids.shape
    capacity = max(2, row_count * top_count // router.shape[1] * 2)
    local_heads = queries.shape[1] // HEAD_DIM
    one_each = operands[9].shape[0] == 1 and lax.axis_size("attn") == 4
    if capacity >= row_count and one_each and local_heads <= HEADS // KV_HEADS:
        return dense_layer(*operands)
    return routed_layer(*operands)


def solution(mesh):
    placed = (
        P(("group", "attn"), ("sect", "pair")),
        P("sect", ("group", "attn"), None, None),
        P(("group", "attn"), None),
        P(("group", "attn")),
        P(("sect", "pair"), "attn"),
        P(("group", "attn", "sect", "pair"), None),
        P(),
        P(),
        P(("group", "attn", "sect", "pair"), None),
        P(("attn", "pair"), None, "sect"),
        P(("attn", "pair"), None, "sect"),
        P(("attn", "pair"), None, "sect"),
    )
    return jax.shard_map(
        on_device,
        mesh=mesh,
        in_specs=placed,
        out_specs=P(("group", "attn", "sect", "pair"), None),
        check_vma=False,
    )
```

```python
import functools
import math

import jax
import jax.numpy as jnp
from jax import lax
from jax.experimental import pallas as pl
from jax.experimental.pallas import tpu as pltpu
from jax.sharding import PartitionSpec as P


HEADS = 32
KV_HEADS = 4
HEAD_DIM = 128


VMEM = pl.BlockSpec(memory_space=pltpu.VMEM)


def routed_layer(
    queries,
    kv_pool,
    block_list,
    cache_len,
    out_weight,
    residual,
    norm_gain,
    router,
    expert_ids,
    w_gate,
    w_up,
    w_down,
):
    head_dim = HEAD_DIM
    per_kv = HEADS // KV_HEADS
    group_rows, head_cols = queries.shape
    local_heads = head_cols // head_dim
    pool_all = lax.all_gather(kv_pool, "attn", axis=1, tiled=True)
    picked = jnp.take(pool_all, block_list[0], axis=1)
    kv_local = lax.axis_index("pair") * local_heads // per_kv
    chosen = lax.dynamic_index_in_dim(picked, kv_local, 0, keepdims=False)
    chosen = chosen.reshape(-1, 2 * head_dim)
    key_rows = chosen[:, :head_dim]
    values = chosen[:, head_dim:]
    query_heads = queries.reshape(group_rows, local_heads, head_dim)
    scores = jnp.einsum(
        "rhd,td->rht", query_heads, key_rows, preferred_element_type=jnp.float32
    ) / math.sqrt(head_dim)
    live_mask = jnp.arange(key_rows.shape[0]) < cache_len[0]
    scores = jnp.where(live_mask, scores, -jnp.inf)
    row_top = jnp.max(scores, axis=-1, keepdims=True)
    lifted = jnp.exp(scores - row_top)
    row_total = jnp.sum(lifted, axis=-1)
    soft_weights = lifted.astype(jnp.bfloat16)
    mixed_heads = (
        jnp.einsum("rht,td->rhd", soft_weights, values, preferred_element_type=jnp.float32)
        / row_total[..., None]
    )
    attended = mixed_heads.reshape(group_rows, head_cols).astype(jnp.bfloat16)
    partial_value = jnp.dot(
        attended,
        lax.all_gather(out_weight, "attn", axis=1, tiled=True),
        preferred_element_type=jnp.float32,
    )
    summed = lax.psum_scatter(partial_value, ("sect", "pair"), scatter_dimension=0, tiled=True)
    mixed_f32 = residual.astype(jnp.float32) + summed
    mixed_rows = mixed_f32.astype(jnp.bfloat16)
    mixed_f32 = mixed_rows.astype(jnp.float32)
    normed = (
        mixed_f32
        * lax.rsqrt(jnp.mean(mixed_f32 * mixed_f32, axis=-1, keepdims=True) + 1e-06)
        * norm_gain
    ).astype(jnp.bfloat16)
    logits = jnp.dot(normed, router, preferred_element_type=jnp.float32)
    chosen_logits = jnp.take_along_axis(logits, expert_ids, axis=1)
    route_weights = jax.nn.softmax(chosen_logits, axis=-1)
    row_count, top_count = expert_ids.shape
    expert_count = router.shape[1]
    model_width = residual.shape[1]
    capacity = max(2, row_count * top_count // expert_count * 2)
    flat_ids = expert_ids.reshape(-1)
    onehot = (flat_ids[:, None] == jnp.arange(expert_count, dtype=jnp.int32)[None, :]).astype(
        jnp.int32
    )
    earlier = jnp.cumsum(onehot, axis=0) - onehot
    slot_index = jnp.sum(earlier * onehot, axis=1)
    source = jnp.repeat(jnp.arange(row_count, dtype=jnp.int32), top_count)
    outgoing = (
        jnp.zeros((expert_count, capacity, model_width), jnp.bfloat16)
        .at[flat_ids, slot_index]
        .set(normed[source])
    )
    received = lax.all_to_all(outgoing, ("attn", "pair"), split_axis=0, concat_axis=0, tiled=True)
    sections = lax.axis_size("sect")
    every_section = lax.all_gather(received, "sect", axis=0, tiled=True)
    tokens_in = every_section.reshape(-1, model_width)
    gate_val = jnp.dot(tokens_in, w_gate[0], preferred_element_type=jnp.float32)
    up_val = jnp.dot(tokens_in, w_up[0], preferred_element_type=jnp.float32)
    part_hidden = (jax.nn.silu(gate_val) * up_val).astype(jnp.bfloat16)
    hidden = lax.all_gather(part_hidden, "sect", axis=1, tiled=True)
    out_slice = jnp.dot(hidden, w_down[0], preferred_element_type=jnp.float32).astype(jnp.bfloat16)
    out_slice = out_slice.reshape(sections, expert_count, capacity, model_width // sections)
    segmented = lax.all_to_all(out_slice, "sect", split_axis=0, concat_axis=3, tiled=True)
    returned = lax.all_to_all(
        segmented[0], ("attn", "pair"), split_axis=0, concat_axis=0, tiled=True
    )
    gathered = (
        returned[flat_ids, slot_index]
        .reshape(row_count, top_count, model_width)
        .astype(jnp.float32)
    )
    joined = jnp.sum(route_weights[:, :, None] * gathered, axis=1)
    return (mixed_f32 + joined).astype(jnp.bfloat16)


def rotate(value, axis, step):
    size = lax.axis_size(axis)
    return lax.ppermute(value, axis, [(i, (i + step) % size) for i in range(size)])


def swap(value, axis, mask):
    size = lax.axis_size(axis)
    return lax.ppermute(value, axis, [(i, i ^ mask) for i in range(size)])


def anchor_kernel(out_ref):
    out_ref[...] = jnp.zeros_like(out_ref)


def pack_kernel(attn, sect, *refs):
    _, kv_ref, list_ref, len_ref, res_ref, ids_ref, down_ref, *refs = refs
    own_ref, far_ref, near_ref, *downs = refs
    my_attn, my_sect = lax.axis_index("attn"), lax.axis_index("sect")
    ff = downs[0].shape[0]
    for i in range(sect):
        start = pl.multiple_of(lax.rem(my_sect + i, sect) * ff, ff)
        downs[i][...] = down_ref[pl.ds(start, ff), :]
    per_dev = res_ref.shape[0]
    top = ids_ref.shape[0]
    width = res_ref.shape[1] // attn
    _, blocks, keys, kv_cols = kv_ref.shape
    folds = width // kv_cols
    local_heads = HEADS // (lax.axis_size("sect") * lax.axis_size("pair"))
    kv_local = lax.axis_index("pair") * local_heads // (HEADS // KV_HEADS)
    lane = lax.broadcasted_iota(jnp.int32, (per_dev, kv_cols - 128), 1)
    facts = jnp.zeros((per_dev, kv_cols - 128), jnp.int32)
    list_len = list_ref.shape[1]
    for j in range(list_len):
        facts = jnp.where(lane == j, list_ref[:, j : j + 1], facts)
    length = jnp.broadcast_to(len_ref[...], (per_dev, 1))
    facts = jnp.where(lane == list_len, length // 128, facts)
    facts = jnp.where(lane == list_len + 1, lax.rem(length, 128), facts)
    facts = facts.astype(jnp.float32).astype(jnp.bfloat16)
    eye = (
        lax.broadcasted_iota(jnp.int32, (per_dev, per_dev), 0)
        == lax.broadcasted_iota(jnp.int32, (per_dev, per_dev), 1)
    )
    ids = lax.dot_general(
        eye.astype(jnp.float32).astype(jnp.bfloat16),
        ids_ref[...].astype(jnp.float32).astype(jnp.bfloat16),
        (((1,), (1,)), ((), ())),
        preferred_element_type=jnp.float32,
    )
    ids = jnp.concatenate([ids, jnp.zeros((per_dev, 128 - top), jnp.float32)], axis=1)
    named = jnp.concatenate([ids.astype(jnp.bfloat16), facts], axis=1)

    def put_slice(ref, row, receiver):
        for f in range(folds):
            start = pl.multiple_of(receiver * width + f * kv_cols, kv_cols)
            ref[row + f * per_dev : row + (f + 1) * per_dev, :] = res_ref[:, pl.ds(start, kv_cols)]

    first = folds * per_dev
    after = first + blocks * keys
    for ref, mask in ((own_ref, 0), (far_ref, 2), (near_ref, 1)):
        put_slice(ref, 0, my_attn ^ mask)
        for b in range(blocks):
            ref[first + b * keys : first + (b + 1) * keys, :] = kv_ref[kv_local, b]
        ref[after : after + per_dev, :] = named
    put_slice(far_ref, after + per_dev, my_attn ^ 3)


def attend_kernel(attn, sect, pair, list_len, blocks, keys, *refs):
    q_refs, refs = refs[:attn], refs[attn:]
    pack_refs, refs = refs[:attn], refs[attn:]
    w_ref, refs = refs[0], refs[1:]
    part_refs, refs = refs[:pair], refs[pair:]
    ids_ref, pool, attended, split = refs
    per_dev = ids_ref.shape[0]
    rows, head_cols = q_refs[0].shape
    kv_cols = pack_refs[0].shape[1]
    width = w_ref.shape[1]
    heads = head_cols // HEAD_DIM
    folds = width // kv_cols
    me, my_sect, my_pair = (lax.axis_index(n) for n in ("attn", "sect", "pair"))
    lane = lax.broadcasted_iota(jnp.int32, (1, kv_cols - 128), 1)
    cache_at = [0 if k == 3 else folds * per_dev for k in range(attn)]
    named_at = [at + blocks * keys for at in cache_at]
    slice_at = [named_at[k] + per_dev if k == 3 else 0 for k in range(attn)]
    lists, lives = [], []
    for k in range(attn):
        group = me ^ k
        for b in range(blocks):
            at = cache_at[k] + b * keys
            pool[group * blocks + b] = pack_refs[k][at : at + keys, :]
        facts = pack_refs[k][named_at[k] : named_at[k] + per_dev, 128:]
        facts = facts.astype(jnp.float32)[0:1, :]

        def fact(j, facts=facts):
            return jnp.sum(jnp.where(lane == j, facts, 0.0)).astype(jnp.int32)

        lists.append([fact(j) for j in range(list_len)])
        lives.append(fact(list_len) * 128 + fact(list_len + 1))
    for k in range(attn):
        group = me ^ k
        picked = [pool[index] for index in lists[k]]
        key_rows = jnp.concatenate([p[:, :HEAD_DIM] for p in picked], axis=0)
        values = jnp.concatenate([p[:, HEAD_DIM:] for p in picked], axis=0)
        q_all = q_refs[k][...]
        stacked = jnp.concatenate(
            [q_all[:, h * HEAD_DIM : (h + 1) * HEAD_DIM] for h in range(heads)], axis=0
        )
        scores = lax.dot_general(
            stacked, key_rows, (((1,), (1,)), ((), ())), preferred_element_type=jnp.float32
        ) / math.sqrt(HEAD_DIM)
        where = lax.broadcasted_iota(jnp.int32, scores.shape, 1)
        scores = jnp.where(where < lives[k], scores, -jnp.inf)
        top = jnp.max(scores, axis=-1, keepdims=True)
        lifted = jnp.exp(scores - top)
        total = jnp.sum(lifted, axis=-1, keepdims=True)
        mixed = (
            jnp.dot(lifted.astype(jnp.bfloat16), values, preferred_element_type=jnp.float32)
            / total
        ).astype(jnp.bfloat16)
        start = pl.multiple_of(group * rows, rows)
        for h in range(heads):
            attended[pl.ds(start, rows), h * HEAD_DIM : (h + 1) * HEAD_DIM] = mixed[
                h * rows : (h + 1) * rows, :
            ]
    product = jnp.dot(attended[...], w_ref[...], preferred_element_type=jnp.float32)
    for g in range(attn):
        for s in range(sect):
            for p in range(pair):
                source = g * rows + (s * pair + p) * per_dev
                target = (s * attn + g) * per_dev
                split[p, target : target + per_dev, :] = product[source : source + per_dev, :]
    for k in range(attn):
        group = me ^ k
        target = pl.ds(pl.multiple_of((my_sect * attn + group) * per_dev, per_dev), per_dev)
        for f in range(folds):
            at = slice_at[k] + f * per_dev
            split[my_pair, target, f * kv_cols : (f + 1) * kv_cols] += pack_refs[k][
                at : at + per_dev, :
            ].astype(jnp.float32)
        lanes = pl.ds(pl.multiple_of(group * 128, 128), 128)
        ids_ref[:, lanes] = pack_refs[k][named_at[k] : named_at[k] + per_dev, :128]
    for i in range(pair):
        part_refs[i][...] = split[lax.rem(my_pair + i, pair)]


def pair_sum_kernel(sect, pair, kept_ref, *refs):
    came, ids_ref, refs = refs[: pair - 1], refs[pair - 1], refs[pair:]
    totals, sents = refs[:sect], refs[sect:]
    my_sect = lax.axis_index("sect")
    part = kept_ref.shape[0] // sect
    for i in range(sect):
        rows = pl.ds(pl.multiple_of(lax.rem(my_sect + i, sect) * part, part), part)
        total = kept_ref[rows, :]
        for ref in came:
            total = total + ref[rows, :]
        totals[i][...] = total
        sents[i][:part, :] = total.astype(jnp.bfloat16)
    named = ids_ref.shape[1]
    sents[0][part:, :named] = ids_ref[...]
    if named < kept_ref.shape[1]:
        sents[0][part:, named:] = jnp.zeros(
            (ids_ref.shape[0], kept_ref.shape[1] - named), jnp.bfloat16
        )


def sect_sum_kernel(kept_ref, names_ref, *refs):
    *came, mixed_ref, sent_ref = refs
    part = kept_ref.shape[0]
    total = kept_ref[...]
    for ref in came:
        total = total + ref[:part, :].astype(jnp.float32)
    mixed = total.astype(jnp.bfloat16)
    mixed_ref[...] = mixed
    sent_ref[:part, :] = mixed
    sent_ref[part:, :] = names_ref[part:, :]


def expert_kernel(attn, sect, pair, per_dev, top, *refs):
    piece_refs, refs = refs[: attn * pair], refs[attn * pair :]
    gain_ref, router_ref, gate_ref, up_ref, refs = *refs[:4], refs[4:]
    down_refs, refs = refs[:sect], refs[sect:]
    part_refs, refs = refs[:pair], refs[pair:]
    own_refs, (ids_all, contribution) = refs[:-2], refs[-2:]
    part = attn * per_dev
    width = piece_refs[0].shape[1]
    model = width * attn
    me, my_sect, my_pair = (lax.axis_index(n) for n in ("attn", "sect", "pair"))
    my_expert = me * pair + my_pair
    rows = part * pair
    values = []
    squares = jnp.zeros((rows, 1), jnp.float32)
    for k in range(attn):
        value = jnp.concatenate(
            [piece_refs[j * attn + k][:part, :] for j in range(pair)], axis=0
        ).astype(jnp.float32)
        values.append(value)
        squares = squares + jnp.sum(value * value, axis=-1, keepdims=True)
    scale = lax.rsqrt(squares / model + 1e-06)
    gate = up = logits = None
    own_start = pl.multiple_of(me * per_dev, per_dev)
    for k in range(attn):
        group = me ^ k
        cols = pl.ds(pl.multiple_of(group * width, width), width)
        lines = width // 128
        gain = jnp.concatenate(
            [gain_ref[pl.ds(group * lines + j, 1), :] for j in range(lines)], axis=1
        )
        normed = (values[k] * scale * gain).astype(jnp.bfloat16)
        parts = [
            jnp.dot(normed, ref[cols, :], preferred_element_type=jnp.float32)
            for ref in (gate_ref, up_ref)
        ] + [
            lax.dot_general(
                normed,
                router_ref[:, cols],
                (((1,), (1,)), ((), ())),
                preferred_element_type=jnp.float32,
            )
        ]
        if k == 0:
            gate, up, logits = parts
        else:
            gate, up, logits = gate + parts[0], up + parts[1], logits + parts[2]
        for own_ref in own_refs:
            own_ref[:, cols] = piece_refs[k][pl.ds(own_start, per_dev), :]
    for j in range(pair):
        block = piece_refs[j * attn][part:, :].astype(jnp.float32)
        for g in range(attn):
            target = j * part + g * per_dev
            ids_all[target : target + per_dev, :] = block[:, g * 128 : g * 128 + top]
    ids = ids_all[...]
    lane = lax.broadcasted_iota(jnp.int32, logits.shape, 1)
    lane_f = lane.astype(jnp.float32)
    named = lane < 0
    for c in range(top):
        named = named | (ids[:, c : c + 1] == lane_f)
    chosen = jnp.where(named, logits, -jnp.inf)
    lifted = jnp.exp(chosen - jnp.max(chosen, axis=-1, keepdims=True))
    weights = lifted / jnp.sum(lifted, axis=-1, keepdims=True)
    weight = jnp.sum(jnp.where(lane == my_expert, weights, 0.0), axis=-1, keepdims=True)
    hidden = (gate / (1.0 + jnp.exp(-gate)) * up).astype(jnp.bfloat16)
    columns = down_refs[0].shape[1]
    for i in range(sect):
        from_sect = lax.rem(my_sect + sect - i, sect)
        cols = pl.ds(pl.multiple_of(from_sect * columns, columns), columns)
        contribution[:, cols] = (
            jnp.dot(hidden, down_refs[i][...], preferred_element_type=jnp.float32) * weight
        )
    part_refs[0][...] = contribution[:part, :]
    for j in range(1, pair):
        part_refs[j][...] = contribution[j * part : (j + 1) * part, :].astype(jnp.bfloat16)


def sum_kernel(kept_ref, *refs):
    *came, out_ref = refs
    total = kept_ref[...]
    for ref in came:
        total = total + ref[...].astype(jnp.float32)
    out_ref[...] = total.astype(out_ref.dtype)


def split_kernel(attn, kept_ref, *refs):
    came, outs = refs[:-attn], refs[-attn:]
    me = lax.axis_index("attn")
    part = kept_ref.shape[0] // attn
    for i in range(attn):
        rows = pl.ds(pl.multiple_of((me ^ i) * part, part), part)
        total = kept_ref[rows, :]
        for ref in came:
            total = total + ref[rows, :].astype(jnp.float32)
        outs[i][...] = total.astype(outs[i].dtype)


def call(kernel, operands, outs, scratch=(), limit=4 << 20, flops=1 << 20):
    moved = sum(x.size * x.dtype.itemsize for x in operands)
    return pl.pallas_call(
        kernel,
        out_shape=outs,
        in_specs=[VMEM] * len(operands),
        out_specs=jax.tree.map(lambda _: VMEM, outs),
        scratch_shapes=list(scratch),
        compiler_params=pltpu.CompilerParams(vmem_limit_bytes=limit),
        cost_estimate=pl.CostEstimate(flops=flops, bytes_accessed=moved, transcendentals=0),
    )(*operands)


def dense_layer(
    queries,
    kv_pool,
    block_list,
    cache_len,
    out_weight,
    residual,
    norm_gain,
    router,
    expert_ids,
    w_gate,
    w_up,
    w_down,
):
    attn, sect, pair = (lax.axis_size(n) for n in ("attn", "sect", "pair"))
    bf16, f32 = jnp.bfloat16, jnp.float32
    shape = jax.ShapeDtypeStruct
    rows, head_cols = queries.shape
    per_dev, model = residual.shape
    top = expert_ids.shape[1]
    width = out_weight.shape[1]
    ff = w_gate.shape[2]
    list_len = block_list.shape[1]
    _, blocks, keys, kv_cols = kv_pool.shape
    half = attn * sect * per_dev
    slice_rows = per_dev * width // kv_cols
    packed = slice_rows + blocks * keys + per_dev

    anchor = call(anchor_kernel, [], shape((8, 128), f32), flops=1 << 34)
    far_q = swap(queries, "attn", 2)
    near_q = swap(queries, "attn", 1)
    own_pack, far_pack, near_pack, *downs = call(
        functools.partial(pack_kernel, attn, sect),
        [
            anchor,
            kv_pool,
            block_list,
            cache_len,
            residual,
            expert_ids.T,
            w_down[0],
        ],
        [
            shape((packed, kv_cols), bf16),
            shape((packed + slice_rows, kv_cols), bf16),
            shape((packed, kv_cols), bf16),
        ]
        + [shape((ff, w_down.shape[2]), bf16)] * sect,
    )
    far_pack = swap(far_pack, "attn", 2)
    downs = [downs[0]] + [rotate(downs[i], "sect", i) for i in range(1, sect)]
    near_pack = swap(near_pack, "attn", 1)
    last_pack = swap(far_pack[slice_rows:], "attn", 1)
    last_q = swap(far_q, "attn", 1)
    q = [queries, near_q, far_q, last_q]
    packs = [own_pack, near_pack, far_pack, last_pack]

    parts = call(
        functools.partial(
            attend_kernel, attn, sect, pair, list_len, blocks, keys
        ),
        q + packs + [out_weight],
        [shape((half, width), f32)] * pair + [shape((per_dev, attn * 128), bf16)],
        [
            pltpu.VMEM((attn * blocks, keys, kv_cols), bf16),
            pltpu.VMEM((attn * rows, head_cols), bf16),
            pltpu.VMEM((pair, half, width), f32),
        ],
        limit=16 << 20,
    )
    part = attn * per_dev
    sums = call(
        functools.partial(pair_sum_kernel, sect, pair),
        [parts[0]]
        + [rotate(parts[j], "pair", j) for j in range(1, pair)]
        + [parts[pair]],
        [shape((part, width), f32)] * sect
        + [shape((part + per_dev, width), bf16)]
        + [shape((part, width), bf16)] * (sect - 1),
    )
    totals, sents = sums[:sect], sums[sect:]
    theirs = [rotate(sents[0], "sect", sect - i) for i in range(1, sect)]
    mine = [rotate(sents[i], "sect", i) for i in range(1, sect)]
    operands = [norm_gain.reshape(-1, 128), router.T, w_gate[0], w_up[0]] + downs

    def experts(shift):
        if shift == 0:
            names, came = sents[0], mine
        else:
            names, came = theirs[shift - 1], [theirs[shift - 1]]
        mixed, named = call(
            sect_sum_kernel,
            [totals[shift], names] + came,
            [shape((part, width), bf16), shape((part + per_dev, width), bf16)],
        )
        piece = {0: named}
        for k in range(1, attn):
            piece[k] = swap(mixed, "attn", k)
        pieces = [piece[k] for k in range(attn)]
        for j in range(1, pair):
            pieces += [rotate(piece[k], "pair", j) for k in range(attn)]
        outs = call(
            functools.partial(expert_kernel, attn, sect, pair, per_dev, top),
            pieces + operands,
            [shape((part, model), f32)]
            + [shape((part, model), bf16)] * (pair - 1)
            + [shape((per_dev, model), bf16)] * (shift == 0),
            [pltpu.VMEM((part * pair, top), f32), pltpu.VMEM((part * pair, model), f32)],
            limit=16 << 20,
            flops=1 << 31,
        )
        came = [rotate(outs[j], "pair", pair - j) for j in range(1, pair)]
        return outs, came

    def reduced(shift):
        outs, came = experts(shift)
        sums = call(
            functools.partial(split_kernel, attn),
            [outs[0]] + came,
            [shape((per_dev, model), f32)] + [shape((per_dev, model), bf16)] * (attn - 1),
        )
        home = [swap(sums[k], "attn", k) for k in range(1, attn)]
        return outs, sums[0], home

    from_sect = []
    for i in range(1, sect):
        _, own, home = reduced(i)
        sent = call(sum_kernel, [own] + home, shape((per_dev, model), bf16))
        from_sect.append(rotate(sent, "sect", i))
    outs, own, home = reduced(0)
    total = outs[pair].astype(f32) + own
    for came in home + from_sect:
        total = total + came.astype(f32)
    return total.astype(bf16)


def on_device(*operands):
    queries, expert_ids, router = operands[0], operands[8], operands[7]
    row_count, top_count = expert_ids.shape
    capacity = max(2, row_count * top_count // router.shape[1] * 2)
    local_heads = queries.shape[1] // HEAD_DIM
    one_each = operands[9].shape[0] == 1
    sizes = tuple(lax.axis_size(n) for n in ("attn", "sect", "pair"))
    exchanged = sizes == (4, 2, 2) and local_heads <= HEADS // KV_HEADS
    if capacity >= row_count and one_each and exchanged:
        return dense_layer(*operands)
    return routed_layer(*operands)


def solution(mesh):
    placed = (
        P(("group", "attn"), ("sect", "pair")),
        P("sect", ("group", "attn"), None, None),
        P(("group", "attn"), None),
        P(("group", "attn")),
        P(("sect", "pair"), "attn"),
        P(("group", "attn", "sect", "pair"), None),
        P(),
        P(),
        P(("group", "attn", "sect", "pair"), None),
        P(("attn", "pair"), None, "sect"),
        P(("attn", "pair"), None, "sect"),
        P(("attn", "pair"), None, "sect"),
    )
    return jax.shard_map(
        on_device,
        mesh=mesh,
        in_specs=placed,
        out_specs=P(("group", "attn", "sect", "pair"), None),
        check_vma=False,
    )
```
